512 devices in a mesh: tm: 64 (over x, z), space: 8 (over y, core).
Axes of the slice: x: 4, y: 4, z: 16, core: 2. Of those that a mesh axis runs over, the one named last changes fastest.
Arguments:
- traj: float32 [64, 32, 128, 128], P('tm', None, 'space'), may hold values from -6 to 6
- start_state: float32 [32, 128, 128], P(None, 'space'), may hold values from -6 to 6
- actions: float32 [64, 16], P('tm'), may hold values from -6 to 6
- hidden_w: bfloat16 [3, 9, 32, 32], replicated, may hold values from -0.375 to 0.375
- hidden_b: float32 [3, 32], replicated, may hold values from -3 to 3
- head_w: bfloat16 [9, 64, 32], replicated, may hold values from -0.375 to 0.375
- cand_b: float32 [32], replicated, may hold values from -3 to 3
- gate_b: float32 [32], replicated, may hold values from 0 to 9
- skip: float32 [32], replicated, may hold values from 0.1 to 0.9
- act_proj: float32 [16, 64], replicated, may hold values from -1.5 to 1.5
Outputs:
- new_traj: float32 [64, 32, 128, 128], P('tm', None, 'space')
- res_msq: float32 [64], P('tm')
The draws below stay inside these ranges and needn't reach their ends.
All inputs are finite; a program needn't handle non-finite values.
Results may differ from the reference program's by a relative error of at most 0.0015.
Values may be sent and summed in bfloat16 or wider, within the bound.
No kernel may reach another device: no remote copies, remote signals or barrier semaphores. Data moves between devices by JAX's collectives and lax.ppermute only.
A program may use at most 128 MiB of HBM per device.

```python
import jax
import jax.numpy as jnp
from jax import lax

C = 32
W = 128
ACT = 16
HID_LAYERS = 3
STEPS_DEV = 1
HORIZON = 64
ROWS = 128
N_TM = 64


def level_of(rng, dims, cuts, least, top_value):
    def one(axis_at, blocks):
        draws = jax.random.uniform(jax.random.fold_in(jax.random.fold_in(rng, 6), axis_at), (blocks,), jnp.float32, least / len(cuts), top_value / len(cuts))
        return jnp.repeat(jnp.exp(draws), dims[axis_at] // blocks).reshape((-1,) + (1,) * (len(dims) - axis_at - 1))

    factor_of = one(*cuts[0])
    for cut in cuts[1:]:
        factor_of = factor_of * one(*cut)
    return factor_of


def normal_values(key, dims, deviation, limit, split=(), kind=jnp.bfloat16):
    entries = jax.random.normal(key, dims, jnp.float32) * deviation
    if len(split) > 0:
        entries = level_of(key, dims, split, -0.22, 0.18) * entries
    return jnp.clip(entries, min=-limit, max=limit).astype(kind)


def setup_inputs(seed: int = 0) -> dict:
    keys = jax.random.split(jax.random.key(seed), 11)
    return {
        "traj": normal_values(keys[0], (HORIZON, C, ROWS, W), 1.0, 6.0, ((0, 64), (2, 8)), jnp.float32),
        "start_state": normal_values(keys[1], (C, ROWS, W), 1.0, 6.0, ((1, 8),), jnp.float32),
        "actions": normal_values(keys[2], (HORIZON, ACT), 1.0, 6.0, ((0, 64),), jnp.float32),
        "hidden_w": normal_values(keys[3], (HID_LAYERS, 9, C, C), (9 * C) ** -0.5, 0.375),
        "hidden_b": normal_values(keys[4], (HID_LAYERS, C), 0.5, 3.0, (), jnp.float32),
        "head_w": normal_values(keys[5], (9, 2 * C, C), (9 * C) ** -0.5, 0.375),
        "cand_b": normal_values(keys[6], (C,), 0.5, 3.0, (), jnp.float32),
        "gate_b": jnp.clip(jax.random.uniform(keys[7], (C,), jnp.float32, 0.0, 9.0), 0.0, 9.0),
        "skip": jnp.clip(jax.random.uniform(keys[8], (C,), jnp.float32, 0.1, 0.9), 0.1, 0.9),
        "act_proj": normal_values(keys[9], (ACT, 2 * C), ACT ** -0.5, 1.5, (), jnp.float32),
    }


def conv_same(hidden, taps):
    outs = taps.shape[1]
    ins = taps.shape[2]
    kernel = taps.reshape(3, 3, outs, ins).transpose(2, 3, 0, 1)
    return lax.conv_general_dilated(hidden, kernel, (1, 1), ((1, 1), (1, 1)),
                                    dimension_numbers=("NCHW", "OIHW", "NCHW"),
                                    preferred_element_type=jnp.float32)


def dynamics(guess_in, acts, hidden_w, hidden_b, head_w, cand_b, gate_b, skip, act_proj):
    chans = guess_in.shape[1]
    act_terms = jnp.dot(acts, act_proj, precision=lax.Precision.HIGHEST, preferred_element_type=jnp.float32)
    hidden = guess_in.astype(jnp.bfloat16)
    for layer in range(HID_LAYERS):
        pre = conv_same(hidden, hidden_w[layer]) + hidden_b[layer][None, :, None, None]
        if layer == 0:
            pre = pre + act_terms[:, :chans, None, None]
        hidden = jax.nn.silu(pre).astype(jnp.bfloat16)
    head = conv_same(hidden, head_w)
    cand = jnp.tanh(head[:, :chans] + cand_b[None, :, None, None] + skip[None, :, None, None] * guess_in)
    gate = jax.nn.sigmoid(head[:, chans:] + gate_b[None, :, None, None] + act_terms[:, chans:, None, None])
    fval = gate * guess_in + (1.0 - gate) * cand
    jac = gate + (1.0 - gate) * (1.0 - cand * cand) * skip[None, :, None, None]
    return fval, jac


def reference(traj, start_state, actions, hidden_w, hidden_b, head_w, cand_b, gate_b, skip, act_proj):
    steps = STEPS_DEV
    blocks = traj.reshape(N_TM, steps, traj.shape[1], traj.shape[2], traj.shape[3])
    act_blocks = actions.reshape(N_TM, steps, actions.shape[1])

    def block_step(carry, item):
        last, state = carry
        blk, acts = item
        guess_in = jnp.concatenate([last[None], blk[:steps - 1]], axis=0)
        fval, jac = dynamics(guess_in, acts, hidden_w, hidden_b, head_w, cand_b, gate_b, skip, act_proj)
        resid = jnp.mean((blk - fval) ** 2, axis=(1, 2, 3))
        offs = fval - jac * guess_in

        def advance(yval, pair):
            nxt = pair[0] * yval + pair[1]
            return nxt, nxt

        state, ys = lax.scan(advance, state, (jac, offs))
        return (blk[steps - 1], state), (ys, resid)

    _, (ys, resid) = lax.scan(block_step, (start_state, start_state), (blocks, act_blocks))
    return ys.reshape(traj.shape), resid.reshape(actions.shape[0])
```

```python
import jax
import jax.numpy as jnp
from jax import lax
from jax.experimental import pallas as pl
from jax.experimental.pallas import tpu as pltpu
from jax.sharding import PartitionSpec as P

NX = 4
NZ = 16
HALO = 4
GROUP = 6


def column(vec):
    n = vec.shape[1]
    rows = lax.broadcasted_iota(jnp.int32, (n, n), 0)
    cols = lax.broadcasted_iota(jnp.int32, (n, n), 1)
    return jnp.sum(jnp.where(rows == cols, jnp.broadcast_to(vec, (n, n)), 0.0), axis=1, keepdims=True)


def groups_of(rows):
    return [(g, min(GROUP, rows - g)) for g in range(0, rows, GROUP)]


def conv_kernel(
    main_ref, low_ref, high_ref, traj_ref, act_ref, proj_ref, wh_ref, hb_ref, wo_ref, cb_ref, gb_ref, sk_ref,
    maps_ref, res_ref, xa_ref, xb_ref, band_ref, head_ref,
):
    strip = lax.axis_index("space")
    width = main_ref.shape[2]
    chans = main_ref.shape[1]
    rows = main_ref.shape[0]
    lanes = lax.broadcasted_iota(jnp.int32, (chans, width), 1)
    first, last = lanes == 0, lanes == width - 1

    for ref in (xa_ref, xb_ref):
        ref[:, 3 * chans :, :] = jnp.zeros((ref.shape[0], ref.shape[1] - 3 * chans, width), jnp.bfloat16)
    band_ref[...] = jnp.zeros(band_ref.shape, jnp.bfloat16)
    head_ref[...] = jnp.zeros(head_ref.shape, jnp.bfloat16)

    act = column(act_ref[...])
    terms = jnp.sum(act * proj_ref[...], axis=0, keepdims=True)
    biases = [column(hb_ref[l : l + 1, :]) for l in range(3)]
    biases[0] = biases[0] + column(terms[:, :chans])
    gate_bias = column(gb_ref[...]) + column(terms[:, chans:])
    cand_bias = column(cb_ref[...])
    skip = column(sk_ref[...])

    def put(ref, row, value):
        ref[row, :chans, :] = jnp.where(first, 0.0, pltpu.roll(value, 1, 1)).astype(jnp.bfloat16)
        ref[row, chans : 2 * chans, :] = value.astype(jnp.bfloat16)
        ref[row, 2 * chans : 3 * chans, :] = jnp.where(last, 0.0, pltpu.roll(value, width - 1, 1)).astype(jnp.bfloat16)

    for r in range(HALO):
        put(xa_ref, r, low_ref[r].astype(jnp.float32))
        put(xa_ref, HALO + rows + r, high_ref[r].astype(jnp.float32))
    for r in range(rows):
        put(xa_ref, HALO + r, main_ref[r].astype(jnp.float32))

    def product(band, outs, src, g, n):
        k = (n + 2) * 128
        rhs = src[g : g + n + 2].reshape(k, width)
        return jnp.dot(band[: n * outs, :k], rhs, preferred_element_type=jnp.float32)

    top = strip == 0
    bottom = strip == lax.axis_size("space") - 1
    src, dst = xa_ref, xb_ref
    for layer in range(3):
        for r in range(GROUP):
            for a in range(3):
                band_ref[r * chans : (r + 1) * chans, (r + a) * 128 : (r + a + 1) * 128] = wh_ref[layer, a]
        halo = HALO - 1 - layer
        for g, n in groups_of(rows + 2 * halo):
            acc = product(band_ref, chans, src, g, n).reshape(n, chans, width)
            for j in range(n):
                pre = acc[j] + biases[layer]
                value = 0.5 * pre * (1.0 + jnp.tanh(0.5 * pre))
                if g + j < halo:
                    value = jnp.where(top, 0.0, value)
                if g + j >= halo + rows:
                    value = jnp.where(bottom, 0.0, value)
                put(dst, g + j, value)
        src, dst = dst, src

    for r in range(GROUP):
        for a in range(3):
            head_ref[r * 2 * chans : (r + 1) * 2 * chans, (r + a) * 128 : (r + a + 1) * 128] = wo_ref[a]
    total = jnp.zeros((chans, width), jnp.float32)
    for g, n in groups_of(rows):
        acc = product(head_ref, 2 * chans, src, g, n).reshape(n, 2 * chans, width)
        for j in range(n):
            row = g + j
            guess = main_ref[row].astype(jnp.float32)
            cand = jnp.tanh(acc[j, :chans] + cand_bias + skip * guess)
            rest = 1.0 / (1.0 + jnp.exp(acc[j, chans:] + gate_bias))
            slope = (1.0 - cand * cand) * skip
            maps_ref[row, 0] = rest * (1.0 - slope)
            maps_ref[row, 1] = rest * (cand - slope * guess)
            fval = guess + rest * (cand - guess)
            diff = traj_ref[pl.ds(row, chans, stride=rows), :] - fval
            total = total + diff * diff
    res_ref[...] = jnp.sum(total, axis=0, keepdims=True)


def tap_rows(weights, outs):
    lead = weights.shape[:-3]
    chans = weights.shape[-1]
    split = weights.reshape(lead + (3, 3, outs, chans))
    moved = jnp.swapaxes(split, -3, -2).reshape(lead + (3, outs, 3 * chans))
    return jnp.pad(moved, [(0, 0)] * (len(lead) + 2) + [(0, 128 - 3 * chans)])


def body(traj, start_state, actions, hidden_w, hidden_b, head_w, cand_b, gate_b, skip, act_proj):
    _, chans, rows, width = traj.shape
    n_tm, n_space = lax.axis_size("tm"), lax.axis_size("space")
    place = lax.axis_index("tm")
    source = jnp.where(place == n_tm - 1, start_state, traj[0])
    source = jnp.swapaxes(source.astype(jnp.bfloat16), 0, 1)

    def shifted(value, step):
        pairs = [
            (t * n_space + s, (t + 1) % n_tm * n_space + s + step)
            for t in range(n_tm)
            for s in range(n_space)
            if 0 <= s + step < n_space
        ]
        return lax.ppermute(value, ("tm", "space"), pairs)

    main = shifted(source, 0)
    low = shifted(source[rows - HALO :], 1)
    high = shifted(source[:HALO], -1)

    kb = (GROUP + 2) * 128
    maps, partial = pl.pallas_call(
        conv_kernel,
        out_shape=(
            jax.ShapeDtypeStruct((rows, 2, chans, width), jnp.float32),
            jax.ShapeDtypeStruct((1, width), jnp.float32),
        ),
        scratch_shapes=[
            pltpu.VMEM((rows + 2 * HALO, 128, width), jnp.bfloat16),
            pltpu.VMEM((rows + 2 * HALO, 128, width), jnp.bfloat16),
            pltpu.VMEM((GROUP * chans, kb), jnp.bfloat16),
            pltpu.VMEM((GROUP * 2 * chans, kb), jnp.bfloat16),
        ],
        name="dynamics",
    )(
        main, low, high, traj.reshape(chans * rows, width), actions, act_proj,
        tap_rows(hidden_w, chans), hidden_b, tap_rows(head_w, 2 * chans),
        cand_b[None], gate_b[None], skip[None],
    )

    z_groups = [[x * NZ + z for z in range(NZ)] for x in range(NX)]
    x_groups = [[x * NZ + z for x in range(NX)] for z in range(NZ)]
    sent = lax.all_to_all(maps.astype(jnp.float16), "tm", 0, 0, axis_index_groups=z_groups)
    steps = [(1.0 - sent[z, 0].astype(jnp.float32), sent[z, 1].astype(jnp.float32)) for z in range(NZ)]
    block_a, block_b = steps[0]
    for a, b in steps[1:]:
        block_a, block_b = a * block_a, a * block_b + b
    block = jnp.stack([block_a, block_b])
    blocks = lax.all_to_all(
        jnp.broadcast_to(block[None], (NX,) + block.shape), "tm", 0, 0, axis_index_groups=x_groups
    )
    mine = place // NZ
    state = lax.dynamic_index_in_dim(start_state, place % NZ, 1, False)
    for x in range(NX - 1):
        state = jnp.where(x < mine, blocks[x, 0] * state + blocks[x, 1], state)
    states = []
    for a, b in steps:
        states.append(state)
        state = a * state + b
    back = lax.all_to_all(
        jnp.stack(states).astype(jnp.float16), "tm", 0, 0, axis_index_groups=z_groups
    ).astype(jnp.float32)
    new = back - maps[:, 0] * back + maps[:, 1]
    new_traj = jnp.swapaxes(new, 0, 1)[None]

    parts = lax.all_to_all(jnp.broadcast_to(partial[None], (n_space, 1, width)), "space", 0, 0)
    res_msq = jnp.sum(parts).reshape(1) / (chans * rows * width * n_space)
    return new_traj, res_msq


def solution(mesh):
    return jax.shard_map(
        body,
        mesh=mesh,
        in_specs=(
            P("tm", None, "space", None),
            P(None, "space", None),
            P("tm", None),
            P(),
            P(),
            P(),
            P(),
            P(),
            P(),
            P(),
        ),
        out_specs=(P("tm", None, "space", None), P("tm")),
        check_vma=False,
    )
```

```python
import jax
import jax.numpy as jnp
from jax import lax
from jax.experimental import pallas as pl
from jax.experimental.pallas import tpu as pltpu
from jax.sharding import PartitionSpec as P


NX = 4
NZ = 16
HALO = 4
GROUP = 6
LIMIT = 16 * 2**20


def column(vec):
    n = vec.shape[1]
    rows = lax.broadcasted_iota(jnp.int32, (n, n), 0)
    cols = lax.broadcasted_iota(jnp.int32, (n, n), 1)
    return jnp.sum(jnp.where(rows == cols, jnp.broadcast_to(vec, (n, n)), 0.0), axis=1, keepdims=True)


def groups_of(rows):
    return [(g, min(GROUP, rows - g)) for g in range(0, rows, GROUP)]


def rounded(value):
    return value.astype(jnp.bfloat16).astype(jnp.float32)


def send_kernel(traj_ref, start_ref, act_ref, shift_ref, pair_ref, chip_ref, line_ref):
    chans, _ = shift_ref.shape[1:]
    rows = shift_ref.shape[0] - 1
    last = lax.axis_index("tm") == lax.axis_size("tm") - 1
    even = lax.rem(lax.axis_index("space"), 2) == 0
    line_ref[...] = jnp.zeros(line_ref.shape, jnp.float32)
    rest = act_ref[...]
    for part in range(3):
        piece = rounded(rest)
        line_ref[part : part + 1, : piece.shape[1]] = piece
        rest = rest - piece
    shift_ref[rows] = line_ref[...].astype(jnp.bfloat16)

    def guess(r):
        at = pl.ds(r, chans, stride=rows)
        return jnp.where(last, start_ref[at, :], traj_ref[at, :])

    for r in range(rows):
        shift_ref[r] = traj_ref[pl.ds(r, chans, stride=rows), :].astype(jnp.bfloat16)
    for r in range(HALO):
        upper, lower = guess(r), guess(rows - HALO + r)
        pair_ref[r] = jnp.where(even, lower, upper).astype(jnp.bfloat16)
        chip_ref[r] = jnp.where(even, upper, lower).astype(jnp.bfloat16)


def conv_kernel(
    shift_ref, pair_ref, chip_ref, traj_ref, start_ref, proj_ref, wh_ref, hb_ref, wo_ref, cb_ref, gb_ref, sk_ref,
    maps_ref, res_ref, xa_ref, xb_ref, band_ref, head_ref, guess_ref,
):
    strip = lax.axis_index("space")
    step_last = lax.axis_index("tm") == lax.axis_size("tm") - 1
    even = lax.rem(strip, 2) == 0
    chans, width = shift_ref.shape[1:]
    rows = shift_ref.shape[0] - 1
    lanes = lax.broadcasted_iota(jnp.int32, (chans, width), 1)
    first, last = lanes == 0, lanes == width - 1

    for ref in (xa_ref, xb_ref):
        ref[:, 3 * chans :, :] = jnp.zeros((ref.shape[0], ref.shape[1] - 3 * chans, width), jnp.bfloat16)
    band_ref[...] = jnp.zeros(band_ref.shape, jnp.bfloat16)
    head_ref[...] = jnp.zeros(head_ref.shape, jnp.bfloat16)

    parts = shift_ref[rows].astype(jnp.float32)
    line = parts[0:1] + parts[1:2] + parts[2:3]
    act = column(line[:, : proj_ref.shape[0]])
    terms = jnp.sum(act * proj_ref[...], axis=0, keepdims=True)
    biases = [column(hb_ref[l : l + 1, :]) for l in range(3)]
    biases[0] = biases[0] + column(terms[:, :chans])
    gate_bias = column(gb_ref[...]) + column(terms[:, chans:])
    cand_bias = column(cb_ref[...])
    skip = column(sk_ref[...])

    def put(ref, row, value):
        ref[row, :chans, :] = jnp.where(first, 0.0, pltpu.roll(value, 1, 1)).astype(jnp.bfloat16)
        ref[row, chans : 2 * chans, :] = value.astype(jnp.bfloat16)
        ref[row, 2 * chans : 3 * chans, :] = jnp.where(last, 0.0, pltpu.roll(value, width - 1, 1)).astype(jnp.bfloat16)

    for r in range(HALO):
        pair = pair_ref[r].astype(jnp.float32)
        chip = chip_ref[r].astype(jnp.float32)
        put(xa_ref, r, jnp.where(even, chip, pair))
        put(xa_ref, HALO + rows + r, jnp.where(even, pair, chip))
    for r in range(rows):
        at = pl.ds(r, chans, stride=rows)
        guess = jnp.where(step_last, start_ref[at, :], traj_ref[at, :])
        guess_ref[r] = guess
        put(xa_ref, HALO + r, guess)

    def product(band, outs, src, g, n):
        k = (n + 2) * 128
        rhs = src[g : g + n + 2].reshape(k, width)
        return jnp.dot(band[: n * outs, :k], rhs, preferred_element_type=jnp.float32)

    top = strip == 0
    bottom = strip == lax.axis_size("space") - 1
    src, dst = xa_ref, xb_ref
    for layer in range(3):
        for r in range(GROUP):
            for a in range(3):
                band_ref[r * chans : (r + 1) * chans, (r + a) * 128 : (r + a + 1) * 128] = wh_ref[layer, a]
        halo = HALO - 1 - layer
        for g, n in groups_of(rows + 2 * halo):
            acc = product(band_ref, chans, src, g, n).reshape(n, chans, width)
            for j in range(n):
                pre = acc[j] + biases[layer]
                value = 0.5 * pre * (1.0 + jnp.tanh(0.5 * pre))
                if g + j < halo:
                    value = jnp.where(top, 0.0, value)
                if g + j >= halo + rows:
                    value = jnp.where(bottom, 0.0, value)
                put(dst, g + j, value)
        src, dst = dst, src

    for r in range(GROUP):
        for a in range(3):
            head_ref[r * 2 * chans : (r + 1) * 2 * chans, (r + a) * 128 : (r + a + 1) * 128] = wo_ref[a]
    total = jnp.zeros((chans, width), jnp.float32)
    for g, n in groups_of(rows):
        acc = product(head_ref, 2 * chans, src, g, n).reshape(n, 2 * chans, width)
        for j in range(n):
            row = g + j
            guess = guess_ref[row]
            cand = jnp.tanh(acc[j, :chans] + cand_bias + skip * guess)
            rest = 1.0 / (1.0 + jnp.exp(acc[j, chans:] + gate_bias))
            slope = (1.0 - cand * cand) * skip
            maps_ref[row, 0] = rest * (1.0 - slope)
            maps_ref[row, 1] = rest * (cand - slope * guess)
            fval = guess + rest * (cand - guess)
            diff = shift_ref[row].astype(jnp.float32) - fval
            total = total + diff * diff
    res_ref[...] = jnp.sum(total, axis=0, keepdims=True)


def prefix_kernel(maps_ref, pref_ref):
    shape = maps_ref.shape[2:]
    pref_ref[0, 0] = jnp.ones(shape, jnp.float32)
    pref_ref[0, 1] = jnp.zeros(shape, jnp.float32)
    a = 1.0 - maps_ref[0, 0]
    b = maps_ref[0, 1]
    for z in range(1, maps_ref.shape[0]):
        pref_ref[z, 0] = a
        pref_ref[z, 1] = b
        keep = 1.0 - maps_ref[z, 0]
        a, b = keep * a, keep * b + maps_ref[z, 1]


def tap_rows(weights, outs):
    lead = weights.shape[:-3]
    chans = weights.shape[-1]
    split = weights.reshape(lead + (3, 3, outs, chans))
    moved = jnp.swapaxes(split, -3, -2).reshape(lead + (3, outs, 3 * chans))
    return jnp.pad(moved, [(0, 0)] * (len(lead) + 2) + [(0, 128 - 3 * chans)])


def params():
    return pltpu.CompilerParams(vmem_limit_bytes=LIMIT)


def body(traj, start_state, actions, hidden_w, hidden_b, head_w, cand_b, gate_b, skip, act_proj):
    _, chans, rows, width = traj.shape
    n_tm, n_space = lax.axis_size("tm"), lax.axis_size("space")
    place = lax.axis_index("tm")
    mine = place // NZ
    f32, bf16 = jnp.float32, jnp.bfloat16
    flat = traj.reshape(chans * rows, width)
    begin = start_state.reshape(chans * rows, width)

    shift, pair, chip = pl.pallas_call(
        send_kernel,
        out_shape=(
            jax.ShapeDtypeStruct((rows + 1, chans, width), bf16),
            jax.ShapeDtypeStruct((HALO, chans, width), bf16),
            jax.ShapeDtypeStruct((HALO, chans, width), bf16),
        ),
        scratch_shapes=[pltpu.VMEM((chans, width), f32)],
        compiler_params=params(),
        name="sends",
    )(flat, begin, actions)
    shift = lax.ppermute(shift, "tm", [((t + 1) % n_tm, t) for t in range(n_tm)])
    pair = lax.ppermute(pair, "space", [(s, s ^ 1) for s in range(n_space)])
    crossing = [(s, s + 1) for s in range(1, n_space - 1, 2)]
    chip = lax.ppermute(chip, "space", crossing + [(b, a) for a, b in crossing])

    kb = (GROUP + 2) * 128
    maps, partial = pl.pallas_call(
        conv_kernel,
        out_shape=(
            jax.ShapeDtypeStruct((rows, 2, chans, width), f32),
            jax.ShapeDtypeStruct((1, width), f32),
        ),
        scratch_shapes=[
            pltpu.VMEM((rows + 2 * HALO, 128, width), bf16),
            pltpu.VMEM((rows + 2 * HALO, 128, width), bf16),
            pltpu.VMEM((GROUP * chans, kb), bf16),
            pltpu.VMEM((GROUP * 2 * chans, kb), bf16),
            pltpu.VMEM((rows, chans, width), f32),
        ],
        compiler_params=params(),
        name="dynamics",
    )(
        shift, pair, chip, flat, begin, act_proj,
        tap_rows(hidden_w, chans), hidden_b, tap_rows(head_w, 2 * chans),
        cand_b[None], gate_b[None], skip[None],
    )

    z_groups = [[x * NZ + z for z in range(NZ)] for x in range(NX)]
    x_groups = [[x * NZ + z for x in range(NX)] for z in range(NZ)]
    sent = lax.all_to_all(maps.astype(jnp.float16), "tm", 0, 0, axis_index_groups=z_groups)
    for bit in (1, 2):
        partial = partial + lax.ppermute(partial, "space", [(s, s ^ bit) for s in range(n_space)])
    sent, partial = lax.optimization_barrier((sent, partial))

    steps = [(1.0 - sent[z, 0].astype(f32), sent[z, 1].astype(f32)) for z in range(NZ)]
    block_a, block_b = steps[0]
    for a, b in steps[1:]:
        block_a, block_b = a * block_a, a * block_b + b
    final = mine == NX - 1
    block = jnp.stack([jnp.where(final, steps[-1][0], block_a), jnp.where(final, steps[-1][1], block_b)])
    blocks = lax.all_to_all(
        jnp.broadcast_to(block[None], (NX,) + block.shape), "tm", 0, 0, axis_index_groups=x_groups
    )
    pref = pl.pallas_call(
        prefix_kernel,
        out_shape=jax.ShapeDtypeStruct((NZ, 2, chans, width), f32),
        compiler_params=params(),
        cost_estimate=pl.CostEstimate(flops=2**20, bytes_accessed=2**20, transcendentals=0),
        name="prefix",
    )(sent.astype(f32))
    state = lax.dynamic_index_in_dim(start_state, place % NZ, 1, False)
    state = blocks[NX - 1, 0] * state + blocks[NX - 1, 1]
    for x in range(NX - 1):
        state = jnp.where(x < mine, blocks[x, 0] * state + blocks[x, 1], state)
    states = (pref[:, 0] * state + pref[:, 1]).astype(jnp.float16)
    back = lax.all_to_all(states, "tm", 0, 0, axis_index_groups=z_groups)
    partial = partial + lax.ppermute(partial, "space", [(s, s ^ 4) for s in range(n_space)])
    res_msq = jnp.sum(partial).reshape(1) / (chans * rows * width * n_space)
    res_msq = lax.ppermute(res_msq, "tm", [(t, (t + 1) % n_tm) for t in range(n_tm)])
    back, res_msq = lax.optimization_barrier((back, res_msq))
    new_traj = jnp.swapaxes(back.astype(f32), 0, 1)[None]
    return new_traj, res_msq


def solution(mesh):
    return jax.shard_map(
        body,
        mesh=mesh,
        in_specs=(
            P("tm", None, "space", None),
            P(None, "space", None),
            P("tm", None),
            P(),
            P(),
            P(),
            P(),
            P(),
            P(),
            P(),
        ),
        out_specs=(P("tm", None, "space", None), P("tm")),
        check_vma=False,
    )
```

```python
import jax
import jax.numpy as jnp
from jax import lax
from jax.experimental import pallas as pl
from jax.experimental.pallas import tpu as pltpu
from jax.sharding import PartitionSpec as P


NX = 4
NZ = 16
HALO = 4
GROUP = 6
LIMIT = 16 * 2**20


def column(vec):
    n = vec.shape[1]
    rows = lax.broadcasted_iota(jnp.int32, (n, n), 0)
    cols = lax.broadcasted_iota(jnp.int32, (n, n), 1)
    return jnp.sum(jnp.where(rows == cols, jnp.broadcast_to(vec, (n, n)), 0.0), axis=1, keepdims=True)


def groups_of(rows):
    return [(g, min(GROUP, rows - g)) for g in range(0, rows, GROUP)]


def rounded(value):
    return value.astype(jnp.bfloat16).astype(jnp.float32)


def send_kernel(
    traj_hbm, start_hbm, hb_hbm, cb_hbm, gb_hbm, sk_hbm, proj_hbm, act_ref,
    own_ref, pair_ref, chip_ref, guess_ref, cols_ref, line_ref, proj_ref,
    traj_ref, start_ref, hb_ref, cb_ref, gb_ref, sk_ref, sems,
):
    chans, width = own_ref.shape[1:]
    rows = own_ref.shape[0]
    moves = [
        pltpu.make_async_copy(source, target, sems.at[i])
        for i, (source, target) in enumerate(
            (
                (traj_hbm, traj_ref),
                (start_hbm, start_ref),
                (hb_hbm, hb_ref),
                (cb_hbm, cb_ref),
                (gb_hbm, gb_ref),
                (sk_hbm, sk_ref),
                (proj_hbm, proj_ref),
            )
        )
    ]
    for move in moves:
        move.start()
    last = lax.axis_index("tm") == lax.axis_size("tm") - 1
    even = lax.rem(lax.axis_index("space"), 2) == 0
    line_ref[...] = jnp.zeros(line_ref.shape, jnp.float32)
    rest = act_ref[...]
    for part in range(3):
        piece = rounded(rest)
        line_ref[part : part + 1, : piece.shape[1]] = piece
        rest = rest - piece
    pair_ref[HALO] = line_ref[...].astype(jnp.bfloat16)
    for move in moves:
        move.wait()

    def spread(vec):
        return jnp.broadcast_to(column(vec), (chans, width))

    for i in range(3):
        cols_ref[i] = spread(hb_ref[i : i + 1, :])
    cols_ref[3] = spread(cb_ref[...])
    cols_ref[4] = spread(gb_ref[...])
    cols_ref[5] = spread(sk_ref[...])
    for r in range(rows):
        at = pl.ds(r, chans, stride=rows)
        mine = traj_ref[at, :]
        own_ref[r] = mine.astype(jnp.bfloat16)
        guess_ref[r] = jnp.where(last, start_ref[at, :], mine)
    for r in range(HALO):
        upper, lower = guess_ref[r], guess_ref[rows - HALO + r]
        pair_ref[r] = jnp.where(even, lower, upper).astype(jnp.bfloat16)
        chip_ref[r] = jnp.where(even, upper, lower).astype(jnp.bfloat16)


def conv_kernel(
    guess_ref, pair_ref, chip_ref, line_ref, proj_ref, cols_ref, wh_ref, wo_ref,
    maps_ref, xa_ref, xb_ref, band_ref, head_ref,
):
    strip = lax.axis_index("space")
    even = lax.rem(strip, 2) == 0
    rows, chans, width = guess_ref.shape
    lanes = lax.broadcasted_iota(jnp.int32, (chans, width), 1)
    first, last = lanes == 0, lanes == width - 1

    for ref in (xa_ref, xb_ref):
        ref[:, 3 * chans :, :] = jnp.zeros((ref.shape[0], ref.shape[1] - 3 * chans, width), jnp.bfloat16)
    band_ref[...] = jnp.zeros(band_ref.shape, jnp.bfloat16)
    head_ref[...] = jnp.zeros(head_ref.shape, jnp.bfloat16)

    parts = jnp.where(even, line_ref[...], pair_ref[HALO].astype(jnp.float32))
    line = parts[0:1] + parts[1:2] + parts[2:3]
    act = column(line[:, : proj_ref.shape[0]])
    terms = jnp.sum(act * proj_ref[...], axis=0, keepdims=True)
    biases = [cols_ref[0] + column(terms[:, :chans]), cols_ref[1], cols_ref[2]]
    cand_bias = cols_ref[3]
    gate_bias = cols_ref[4] + column(terms[:, chans:])
    skip = cols_ref[5]

    def put(ref, row, value):
        ref[row, :chans, :] = jnp.where(first, 0.0, pltpu.roll(value, 1, 1)).astype(jnp.bfloat16)
        ref[row, chans : 2 * chans, :] = value.astype(jnp.bfloat16)
        ref[row, 2 * chans : 3 * chans, :] = jnp.where(last, 0.0, pltpu.roll(value, width - 1, 1)).astype(jnp.bfloat16)

    for r in range(HALO):
        pair = pair_ref[r].astype(jnp.float32)
        chip = chip_ref[r].astype(jnp.float32)
        put(xa_ref, r, jnp.where(even, chip, pair))
        put(xa_ref, HALO + rows + r, jnp.where(even, pair, chip))
    for r in range(rows):
        put(xa_ref, HALO + r, guess_ref[r])

    def product(band, outs, src, g, n):
        k = (n + 2) * 128
        rhs = src[g : g + n + 2].reshape(k, width)
        return jnp.dot(band[: n * outs, :k], rhs, preferred_element_type=jnp.float32)

    top = strip == 0
    bottom = strip == lax.axis_size("space") - 1
    src, dst = xa_ref, xb_ref
    for layer in range(3):
        for r in range(GROUP):
            for a in range(3):
                band_ref[r * chans : (r + 1) * chans, (r + a) * 128 : (r + a + 1) * 128] = wh_ref[layer, a]
        halo = HALO - 1 - layer
        for g, n in groups_of(rows + 2 * halo):
            acc = product(band_ref, chans, src, g, n).reshape(n, chans, width)
            for j in range(n):
                pre = acc[j] + biases[layer]
                value = 0.5 * pre * (1.0 + jnp.tanh(0.5 * pre))
                if g + j < halo:
                    value = jnp.where(top, 0.0, value)
                if g + j >= halo + rows:
                    value = jnp.where(bottom, 0.0, value)
                put(dst, g + j, value)
        src, dst = dst, src

    for r in range(GROUP):
        for a in range(3):
            head_ref[r * 2 * chans : (r + 1) * 2 * chans, (r + a) * 128 : (r + a + 1) * 128] = wo_ref[a]
    for g, n in groups_of(rows):
        acc = product(head_ref, 2 * chans, src, g, n).reshape(n, 2 * chans, width)
        for j in range(n):
            row = g + j
            guess = guess_ref[row]
            cand = jnp.tanh(acc[j, :chans] + cand_bias + skip * guess)
            rest = 1.0 / (1.0 + jnp.exp(acc[j, chans:] + gate_bias))
            slope = (1.0 - cand * cand) * skip
            maps_ref[row, 0] = rest * (1.0 - slope)
            maps_ref[row, 1] = rest * (cand - slope * guess)


def residual_kernel(maps_ref, guess_ref, ahead_ref, res_ref):
    rows, chans, width = guess_ref.shape
    total = jnp.zeros((chans, width), jnp.float32)
    for r in range(rows):
        guess = guess_ref[r]
        fval = guess - maps_ref[r, 0] * guess + maps_ref[r, 1]
        diff = ahead_ref[r].astype(jnp.float32) - fval
        total = total + diff * diff
    res_ref[...] = jnp.sum(total, axis=0, keepdims=True)


def prefix_kernel(maps_ref, pref_ref):
    shape = maps_ref.shape[2:]
    pref_ref[0, 0] = jnp.ones(shape, jnp.float32)
    pref_ref[0, 1] = jnp.zeros(shape, jnp.float32)
    a = 1.0 - maps_ref[0, 0]
    b = maps_ref[0, 1]
    for z in range(1, maps_ref.shape[0]):
        pref_ref[z, 0] = a
        pref_ref[z, 1] = b
        keep = 1.0 - maps_ref[z, 0]
        a, b = keep * a, keep * b + maps_ref[z, 1]


def tap_rows(weights, outs):
    lead = weights.shape[:-3]
    chans = weights.shape[-1]
    split = weights.reshape(lead + (3, 3, outs, chans))
    moved = jnp.swapaxes(split, -3, -2).reshape(lead + (3, outs, 3 * chans))
    return jnp.pad(moved, [(0, 0)] * (len(lead) + 2) + [(0, 128 - 3 * chans)])


def params():
    return pltpu.CompilerParams(vmem_limit_bytes=LIMIT)


def body(traj, start_state, actions, hidden_w, hidden_b, head_w, cand_b, gate_b, skip, act_proj):
    _, chans, rows, width = traj.shape
    n_tm, n_space = lax.axis_size("tm"), lax.axis_size("space")
    place = lax.axis_index("tm")
    mine = place // NZ
    f32, bf16 = jnp.float32, jnp.bfloat16
    flat = traj.reshape(chans * rows, width)
    begin = start_state.reshape(chans * rows, width)

    following = [
        ((t + 1) % n_tm * n_space + s, t * n_space + s) for t in range(n_tm) for s in range(0, n_space, 2)
    ]
    act_next = lax.ppermute(actions, ("tm", "space"), following)
    hbm = pl.BlockSpec(memory_space=pltpu.HBM)
    vmem = pl.BlockSpec(memory_space=pltpu.VMEM)
    own, pair, chip, guess, cols, line, proj = pl.pallas_call(
        send_kernel,
        in_specs=[hbm] * 7 + [vmem],
        out_shape=(
            jax.ShapeDtypeStruct((rows, chans, width), bf16),
            jax.ShapeDtypeStruct((HALO + 1, chans, width), bf16),
            jax.ShapeDtypeStruct((HALO, chans, width), bf16),
            jax.ShapeDtypeStruct((rows, chans, width), f32),
            jax.ShapeDtypeStruct((6, chans, width), f32),
            jax.ShapeDtypeStruct((chans, width), f32),
            jax.ShapeDtypeStruct(act_proj.shape, f32),
        ),
        scratch_shapes=[
            pltpu.VMEM((chans * rows, width), f32),
            pltpu.VMEM((chans * rows, width), f32),
            pltpu.VMEM(hidden_b.shape, f32),
            pltpu.VMEM((1, chans), f32),
            pltpu.VMEM((1, chans), f32),
            pltpu.VMEM((1, chans), f32),
            pltpu.SemaphoreType.DMA((7,)),
        ],
        compiler_params=params(),
        name="sends",
    )(*[
        pltpu.with_memory_space_constraint(value, pltpu.HBM)
        for value in (flat, begin, hidden_b, cand_b[None], gate_b[None], skip[None], act_proj)
    ], act_next)
    pair = lax.ppermute(pair, "space", [(s, s ^ 1) for s in range(n_space)])
    crossing = [(s, s + 1) for s in range(1, n_space - 1, 2)]
    chip = lax.ppermute(chip, "space", crossing + [(b, a) for a, b in crossing])

    kb = (GROUP + 2) * 128
    maps = pl.pallas_call(
        conv_kernel,
        out_shape=jax.ShapeDtypeStruct((rows, 2, chans, width), f32),
        scratch_shapes=[
            pltpu.VMEM((rows + 2 * HALO, 128, width), bf16),
            pltpu.VMEM((rows + 2 * HALO, 128, width), bf16),
            pltpu.VMEM((GROUP * chans, kb), bf16),
            pltpu.VMEM((GROUP * 2 * chans, kb), bf16),
        ],
        compiler_params=params(),
        name="dynamics",
    )(guess, pair, chip, line, proj, cols, tap_rows(hidden_w, chans), tap_rows(head_w, 2 * chans))

    z_groups = [[x * NZ + z for z in range(NZ)] for x in range(NX)]
    x_groups = [[x * NZ + z for x in range(NX)] for z in range(NZ)]
    sent = lax.all_to_all(maps.astype(jnp.float16), "tm", 0, 0, axis_index_groups=z_groups)
    ahead = lax.ppermute(own, "tm", [((t + 1) % n_tm, t) for t in range(n_tm)])
    partial = pl.pallas_call(
        residual_kernel,
        out_shape=jax.ShapeDtypeStruct((1, width), f32),
        compiler_params=params(),
        cost_estimate=pl.CostEstimate(flops=2**19, bytes_accessed=2**20, transcendentals=0),
        name="residual",
    )(maps, guess, ahead)
    for bit in (1, 2):
        partial = partial + lax.ppermute(partial, "space", [(s, s ^ bit) for s in range(n_space)])
    sent, partial = lax.optimization_barrier((sent, partial))

    steps = [(1.0 - sent[z, 0].astype(f32), sent[z, 1].astype(f32)) for z in range(NZ)]
    block_a, block_b = steps[0]
    for a, b in steps[1:]:
        block_a, block_b = a * block_a, a * block_b + b
    final = mine == NX - 1
    block = jnp.stack([jnp.where(final, steps[-1][0], block_a), jnp.where(final, steps[-1][1], block_b)])
    blocks = lax.all_to_all(
        jnp.broadcast_to(block[None], (NX,) + block.shape), "tm", 0, 0, axis_index_groups=x_groups
    )
    pref = pl.pallas_call(
        prefix_kernel,
        out_shape=jax.ShapeDtypeStruct((NZ, 2, chans, width), f32),
        compiler_params=params(),
        cost_estimate=pl.CostEstimate(flops=2**20, bytes_accessed=2**20, transcendentals=0),
        name="prefix",
    )(sent.astype(f32))
    state = lax.dynamic_index_in_dim(start_state, place % NZ, 1, False)
    state = blocks[NX - 1, 0] * state + blocks[NX - 1, 1]
    for x in range(NX - 1):
        state = jnp.where(x < mine, blocks[x, 0] * state + blocks[x, 1], state)
    states = (pref[:, 0] * state + pref[:, 1]).astype(jnp.float16)
    back = lax.all_to_all(states, "tm", 0, 0, axis_index_groups=z_groups)
    homes = []
    for bit in (0, 4):
        pairs = [(t * n_space + s, (t + 1) % n_tm * n_space + (s ^ bit)) for t in range(n_tm) for s in range(n_space)]
        homes.append(lax.ppermute(partial, ("tm", "space"), pairs))
    res_msq = jnp.sum(homes[0] + homes[1]).reshape(1) / (chans * rows * width * n_space)
    back, res_msq = lax.optimization_barrier((back, res_msq))
    new_traj = jnp.swapaxes(back.astype(f32), 0, 1)[None]
    return new_traj, res_msq


def solution(mesh):
    return jax.shard_map(
        body,
        mesh=mesh,
        in_specs=(
            P("tm", None, "space", None),
            P(None, "space", None),
            P("tm", None),
            P(),
            P(),
            P(),
            P(),
            P(),
            P(),
            P(),
        ),
        out_specs=(P("tm", None, "space", None), P("tm")),
        check_vma=False,
    )
```

```python
import jax
import jax.numpy as jnp
from jax import lax
from jax.experimental import pallas as pl
from jax.experimental.pallas import tpu as pltpu
from jax.sharding import PartitionSpec as P


NX = 4
NZ = 16
HALO = 4
GROUP = 6
LIMIT = 16 * 2**20


def column(vec):
    n = vec.shape[1]
    rows = lax.broadcasted_iota(jnp.int32, (n, n), 0)
    cols = lax.broadcasted_iota(jnp.int32, (n, n), 1)
    return jnp.sum(jnp.where(rows == cols, jnp.broadcast_to(vec, (n, n)), 0.0), axis=1, keepdims=True)


def groups_of(rows):
    return [(g, min(GROUP, rows - g)) for g in range(0, rows, GROUP)]


def rounded(value):
    return value.astype(jnp.bfloat16).astype(jnp.float32)


def send_kernel(
    traj_hbm, start_hbm, act_hbm, hb_hbm, cb_hbm, gb_hbm, sk_hbm, proj_hbm, wh_hbm, wo_hbm,
    shift_ref, pair_ref, chip_ref, guess_ref, begin_ref, cols_ref, proj_ref, th_ref, to_ref,
    traj_ref, start_ref, act_ref, hb_ref, cb_ref, gb_ref, sk_ref, wh_ref, wo_ref, line_ref, sems,
):
    rows, chans, width = guess_ref.shape
    moves = [
        pltpu.make_async_copy(source, target, sems.at[i])
        for i, (source, target) in enumerate(
            (
                (traj_hbm, traj_ref),
                (start_hbm, start_ref),
                (act_hbm, act_ref),
                (hb_hbm, hb_ref),
                (cb_hbm, cb_ref),
                (gb_hbm, gb_ref),
                (sk_hbm, sk_ref),
                (proj_hbm, proj_ref),
                (wh_hbm, wh_ref),
                (wo_hbm, wo_ref),
            )
        )
    ]
    for move in moves:
        move.start()
    last = lax.axis_index("tm") == lax.axis_size("tm") - 1
    even = lax.rem(lax.axis_index("space"), 2) == 0
    line_ref[...] = jnp.zeros(line_ref.shape, jnp.float32)
    for move in moves:
        move.wait()
    rest = act_ref[...]
    for part in range(3):
        piece = rounded(rest)
        line_ref[part : part + 1, : piece.shape[1]] = piece
        rest = rest - piece
    shift_ref[rows] = line_ref[...].astype(jnp.bfloat16)

    def spread(vec):
        return jnp.broadcast_to(column(vec), (chans, width))

    for i in range(3):
        cols_ref[i] = spread(hb_ref[i : i + 1, :])
    cols_ref[3] = spread(cb_ref[...])
    cols_ref[4] = spread(gb_ref[...])
    cols_ref[5] = spread(sk_ref[...])
    for r in range(rows):
        at = pl.ds(r, chans, stride=rows)
        mine = traj_ref[at, :]
        shift_ref[r] = mine.astype(jnp.bfloat16)
        guess_ref[r] = jnp.where(last, start_ref[at, :], mine)
    place = lax.rem(lax.axis_index("tm"), NZ)
    begin_ref[...] = start_ref[pl.ds(place, chans, stride=rows), :]
    for r in range(HALO):
        upper, lower = guess_ref[r], guess_ref[rows - HALO + r]
        pair_ref[r] = jnp.where(even, lower, upper).astype(jnp.bfloat16)
        chip_ref[r] = jnp.where(even, upper, lower).astype(jnp.bfloat16)
    for a in range(3):
        for layer in range(3):
            th_ref[layer, a] = tile_of([wh_ref[layer, 3 * a + b].astype(jnp.float32) for b in range(3)])
        to_ref[a] = tile_of([wo_ref[3 * a + b].astype(jnp.float32).T for b in range(3)])


def tile_of(taps):
    outs, chans = taps[0].shape
    pad = jnp.zeros((outs, 128 - 3 * chans), jnp.float32)
    return jnp.concatenate(taps + [pad], axis=1).astype(jnp.bfloat16)


def conv_kernel(
    guess_ref, shift_ref, pair_ref, chip_ref, proj_ref, cols_ref, wh_ref, wo_ref,
    maps_ref, res_ref, xa_ref, xb_ref, band_ref, head_ref,
):
    strip = lax.axis_index("space")
    even = lax.rem(strip, 2) == 0
    rows, chans, width = guess_ref.shape
    lanes = lax.broadcasted_iota(jnp.int32, (chans, width), 1)
    first, last = lanes == 0, lanes == width - 1

    for ref in (xa_ref, xb_ref):
        ref[:, 3 * chans :, :] = jnp.zeros((ref.shape[0], ref.shape[1] - 3 * chans, width), jnp.bfloat16)
    band_ref[...] = jnp.zeros(band_ref.shape, jnp.bfloat16)
    head_ref[...] = jnp.zeros(head_ref.shape, jnp.bfloat16)

    parts = shift_ref[rows].astype(jnp.float32)
    line = parts[0:1] + parts[1:2] + parts[2:3]
    act = column(line[:, : proj_ref.shape[0]])
    terms = jnp.sum(act * proj_ref[...], axis=0, keepdims=True)
    biases = [cols_ref[0] + column(terms[:, :chans]), cols_ref[1], cols_ref[2]]
    cand_bias = cols_ref[3]
    gate_bias = cols_ref[4] + column(terms[:, chans:])
    skip = cols_ref[5]

    def put(ref, row, value):
        ref[row, :chans, :] = jnp.where(first, 0.0, pltpu.roll(value, 1, 1)).astype(jnp.bfloat16)
        ref[row, chans : 2 * chans, :] = value.astype(jnp.bfloat16)
        ref[row, 2 * chans : 3 * chans, :] = jnp.where(last, 0.0, pltpu.roll(value, width - 1, 1)).astype(jnp.bfloat16)

    for r in range(HALO):
        pair = pair_ref[r].astype(jnp.float32)
        chip = chip_ref[r].astype(jnp.float32)
        put(xa_ref, r, jnp.where(even, chip, pair))
        put(xa_ref, HALO + rows + r, jnp.where(even, pair, chip))
    for r in range(rows):
        put(xa_ref, HALO + r, guess_ref[r])

    def product(band, outs, src, g, n):
        k = (n + 2) * 128
        rhs = src[g : g + n + 2].reshape(k, width)
        return jnp.dot(band[: n * outs, :k], rhs, preferred_element_type=jnp.float32)

    top = strip == 0
    bottom = strip == lax.axis_size("space") - 1
    src, dst = xa_ref, xb_ref
    for layer in range(3):
        for r in range(GROUP):
            for a in range(3):
                band_ref[r * chans : (r + 1) * chans, (r + a) * 128 : (r + a + 1) * 128] = wh_ref[layer, a]
        halo = HALO - 1 - layer
        for g, n in groups_of(rows + 2 * halo):
            acc = product(band_ref, chans, src, g, n).reshape(n, chans, width)
            for j in range(n):
                pre = acc[j] + biases[layer]
                value = 0.5 * pre * (1.0 + jnp.tanh(0.5 * pre))
                if g + j < halo:
                    value = jnp.where(top, 0.0, value)
                if g + j >= halo + rows:
                    value = jnp.where(bottom, 0.0, value)
                put(dst, g + j, value)
        src, dst = dst, src

    for r in range(GROUP):
        for a in range(3):
            head_ref[r * 2 * chans : (r + 1) * 2 * chans, (r + a) * 128 : (r + a + 1) * 128] = wo_ref[a]
    total = jnp.zeros((chans, width), jnp.float32)
    for g, n in groups_of(rows):
        acc = product(head_ref, 2 * chans, src, g, n).reshape(n, 2 * chans, width)
        for j in range(n):
            row = g + j
            guess = guess_ref[row]
            cand = jnp.tanh(acc[j, :chans] + cand_bias + skip * guess)
            rest = 1.0 / (1.0 + jnp.exp(acc[j, chans:] + gate_bias))
            slope = (1.0 - cand * cand) * skip
            maps_ref[row, 0] = rest * (1.0 - slope)
            maps_ref[row, 1] = rest * (cand - slope * guess)
            fval = guess + rest * (cand - guess)
            diff = shift_ref[row].astype(jnp.float32) - fval
            total = total + diff * diff
    res_ref[...] = jnp.sum(total, axis=0, keepdims=True)


def prefix_kernel(maps_ref, pref_ref):
    shape = maps_ref.shape[2:]
    pref_ref[0, 0] = jnp.ones(shape, jnp.float32)
    pref_ref[0, 1] = jnp.zeros(shape, jnp.float32)
    a = 1.0 - maps_ref[0, 0]
    b = maps_ref[0, 1]
    for z in range(1, maps_ref.shape[0]):
        pref_ref[z, 0] = a
        pref_ref[z, 1] = b
        keep = 1.0 - maps_ref[z, 0]
        a, b = keep * a, keep * b + maps_ref[z, 1]


def params():
    return pltpu.CompilerParams(vmem_limit_bytes=LIMIT)


def body(traj, start_state, actions, hidden_w, hidden_b, head_w, cand_b, gate_b, skip, act_proj):
    _, chans, rows, width = traj.shape
    n_tm, n_space = lax.axis_size("tm"), lax.axis_size("space")
    place = lax.axis_index("tm")
    mine = place // NZ
    f32, bf16 = jnp.float32, jnp.bfloat16
    flat = traj.reshape(chans * rows, width)
    begin = start_state.reshape(chans * rows, width)

    loaded = (
        flat, begin, actions, hidden_b, cand_b[None], gate_b[None], skip[None], act_proj, hidden_w, jnp.swapaxes(head_w, 1, 2),
    )
    shift, pair, chip, guess, entry, cols, proj, taps, head_taps = pl.pallas_call(
        send_kernel,
        in_specs=[pl.BlockSpec(memory_space=pltpu.HBM)] * len(loaded),
        out_shape=(
            jax.ShapeDtypeStruct((rows + 1, chans, width), bf16),
            jax.ShapeDtypeStruct((HALO, chans, width), bf16),
            jax.ShapeDtypeStruct((HALO, chans, width), bf16),
            jax.ShapeDtypeStruct((rows, chans, width), f32),
            jax.ShapeDtypeStruct((chans, width), f32),
            jax.ShapeDtypeStruct((6, chans, width), f32),
            jax.ShapeDtypeStruct(act_proj.shape, f32),
            jax.ShapeDtypeStruct((3, 3, chans, 128), bf16),
            jax.ShapeDtypeStruct((3, 2 * chans, 128), bf16),
        ),
        scratch_shapes=[
            pltpu.VMEM((chans * rows, width), f32),
            pltpu.VMEM((chans * rows, width), f32),
            pltpu.VMEM(actions.shape, f32),
            pltpu.VMEM(hidden_b.shape, f32),
            pltpu.VMEM((1, chans), f32),
            pltpu.VMEM((1, chans), f32),
            pltpu.VMEM((1, chans), f32),
            pltpu.VMEM(hidden_w.shape, bf16),
            pltpu.VMEM((9, chans, 2 * chans), bf16),
            pltpu.VMEM((chans, width), f32),
            pltpu.SemaphoreType.DMA((len(loaded),)),
        ],
        compiler_params=params(),
        name="sends",
    )(*[pltpu.with_memory_space_constraint(value, pltpu.HBM) for value in loaded])
    crossing = [(s, s + 1) for s in range(1, n_space - 1, 2)]
    shift = lax.ppermute(shift, "tm", [((t + 1) % n_tm, t) for t in range(n_tm)])
    chip = lax.ppermute(chip, "space", crossing + [(b, a) for a, b in crossing])
    pair = lax.ppermute(pair, "space", [(s, s ^ 1) for s in range(n_space)])

    kb = (GROUP + 2) * 128
    maps, partial = pl.pallas_call(
        conv_kernel,
        out_shape=(
            jax.ShapeDtypeStruct((rows, 2, chans, width), f32),
            jax.ShapeDtypeStruct((1, width), f32),
        ),
        scratch_shapes=[
            pltpu.VMEM((rows + 2 * HALO, 128, width), bf16),
            pltpu.VMEM((rows + 2 * HALO, 128, width), bf16),
            pltpu.VMEM((GROUP * chans, kb), bf16),
            pltpu.VMEM((GROUP * 2 * chans, kb), bf16),
        ],
        compiler_params=params(),
        name="dynamics",
    )(guess, shift, pair, chip, proj, cols, taps, head_taps)

    z_groups = [[x * NZ + z for z in range(NZ)] for x in range(NX)]
    x_groups = [[x * NZ + z for x in range(NX)] for z in range(NZ)]
    sent = lax.all_to_all(maps.astype(jnp.float16), "tm", 0, 0, axis_index_groups=z_groups)
    for bit in (1, 2, 4):
        partial = partial + lax.ppermute(partial, "space", [(s, s ^ bit) for s in range(n_space)])
    res_msq = jnp.sum(partial).reshape(1) / (chans * rows * width * n_space)
    flags = [mine == NX - 1] + [x < mine for x in range(NX - 1)]
    sent, res_msq, flags = lax.optimization_barrier((sent, res_msq, flags))

    steps = [(1.0 - sent[z, 0].astype(f32), sent[z, 1].astype(f32)) for z in range(NZ)]
    block_a, block_b = steps[0]
    for a, b in steps[1:]:
        block_a, block_b = a * block_a, a * block_b + b
    block = jnp.stack([jnp.where(flags[0], steps[-1][0], block_a), jnp.where(flags[0], steps[-1][1], block_b)])
    pref = pl.pallas_call(
        prefix_kernel,
        out_shape=jax.ShapeDtypeStruct((NZ, 2, chans, width), f32),
        compiler_params=params(),
        cost_estimate=pl.CostEstimate(flops=2**20, bytes_accessed=2**20, transcendentals=0),
        name="prefix",
    )(sent.astype(f32))
    copies, pref, entry = lax.optimization_barrier((jnp.broadcast_to(block[None], (NX,) + block.shape), pref, entry))
    blocks = lax.all_to_all(copies, "tm", 0, 0, axis_index_groups=x_groups)
    state = blocks[NX - 1, 0] * entry + blocks[NX - 1, 1]
    for x in range(NX - 1):
        state = jnp.where(flags[x + 1], blocks[x, 0] * state + blocks[x, 1], state)
    states = (pref[:, 0] * state + pref[:, 1]).astype(jnp.float16)
    back = lax.all_to_all(states, "tm", 0, 0, axis_index_groups=z_groups)
    res_msq = lax.ppermute(res_msq, "tm", [(t, (t + 1) % n_tm) for t in range(n_tm)])
    back, res_msq = lax.optimization_barrier((back, res_msq))
    new_traj = jnp.swapaxes(back.astype(f32), 0, 1)[None]
    return new_traj, res_msq


def solution(mesh):
    return jax.shard_map(
        body,
        mesh=mesh,
        in_specs=(
            P("tm", None, "space", None),
            P(None, "space", None),
            P("tm", None),
            P(),
            P(),
            P(),
            P(),
            P(),
            P(),
            P(),
        ),
        out_specs=(P("tm", None, "space", None), P("tm")),
        check_vma=False,
    )
```

```python
import jax
import jax.numpy as jnp
from jax import lax
from jax.experimental import pallas as pl
from jax.experimental.pallas import tpu as pltpu
from jax.sharding import PartitionSpec as P


NX = 4
NZ = 16
HALO = 4
GROUP = 6
LIMIT = 16 * 2**20


def column(vec):
    n = vec.shape[1]
    rows = lax.broadcasted_iota(jnp.int32, (n, n), 0)
    cols = lax.broadcasted_iota(jnp.int32, (n, n), 1)
    return jnp.sum(jnp.where(rows == cols, jnp.broadcast_to(vec, (n, n)), 0.0), axis=1, keepdims=True)


def groups_of(rows):
    return [(g, min(GROUP, (rows - g) // 2)) for g in range(0, rows, 2 * GROUP)]


def rounded(value):
    return value.astype(jnp.bfloat16).astype(jnp.float32)


def send_kernel(
    traj_hbm, start_hbm, act_hbm, hb_hbm, cb_hbm, gb_hbm, sk_hbm, proj_hbm, wh_hbm, wo_hbm,
    shift_ref, pair_ref, chip_ref, guess_ref, begin_ref, cols_ref, proj_ref, th_ref, to_ref,
    traj_ref, start_ref, act_ref, hb_ref, cb_ref, gb_ref, sk_ref, wh_ref, wo_ref, line_ref, sems,
):
    rows, chans, width = guess_ref.shape
    moves = [
        pltpu.make_async_copy(source, target, sems.at[i])
        for i, (source, target) in enumerate(
            (
                (traj_hbm, traj_ref),
                (start_hbm, start_ref),
                (act_hbm, act_ref),
                (hb_hbm, hb_ref),
                (cb_hbm, cb_ref),
                (gb_hbm, gb_ref),
                (sk_hbm, sk_ref),
                (proj_hbm, proj_ref),
                (wh_hbm, wh_ref),
                (wo_hbm, wo_ref),
            )
        )
    ]
    for move in moves:
        move.start()
    last = lax.axis_index("tm") == lax.axis_size("tm") - 1
    even = lax.rem(lax.axis_index("space"), 2) == 0
    line_ref[...] = jnp.zeros(line_ref.shape, jnp.float32)
    for move in moves:
        move.wait()
    rest = act_ref[...]
    for part in range(3):
        piece = rounded(rest)
        line_ref[part : part + 1, : piece.shape[1]] = piece
        rest = rest - piece
    shift_ref[rows] = line_ref[...].astype(jnp.bfloat16)

    def spread(vec):
        return jnp.broadcast_to(column(vec), (chans, width))

    for i in range(3):
        cols_ref[i] = spread(hb_ref[i : i + 1, :])
    cols_ref[3] = spread(cb_ref[...])
    cols_ref[4] = spread(gb_ref[...])
    cols_ref[5] = spread(sk_ref[...])
    for r in range(rows):
        at = pl.ds(r, chans, stride=rows)
        mine = traj_ref[at, :]
        shift_ref[r] = mine.astype(jnp.bfloat16)
        guess_ref[r] = jnp.where(last, start_ref[at, :], mine)
    place = lax.rem(lax.axis_index("tm"), NZ)
    begin_ref[...] = start_ref[pl.ds(place, chans, stride=rows), :]
    for r in range(HALO):
        upper, lower = guess_ref[r], guess_ref[rows - HALO + r]
        pair_ref[r] = jnp.where(even, lower, upper).astype(jnp.bfloat16)
        chip_ref[r] = jnp.where(even, upper, lower).astype(jnp.bfloat16)
    for a in range(3):
        for layer in range(3):
            th_ref[layer, a] = tile_of([wh_ref[layer, 3 * a + b].astype(jnp.float32) for b in range(3)])
        to_ref[a] = tile_of([wo_ref[3 * a + b].astype(jnp.float32).T for b in range(3)])


def tile_of(taps):
    outs, chans = taps[0].shape
    pad = jnp.zeros((outs, 128 - 3 * chans), jnp.float32)
    return jnp.concatenate(taps + [pad], axis=1).astype(jnp.bfloat16)


def conv_kernel(
    guess_ref, shift_ref, pair_ref, chip_ref, proj_ref, cols_ref, wh_ref, wo_ref,
    maps_ref, res_ref, xa_ref, xb_ref, band_ref, head_ref,
):
    strip = lax.axis_index("space")
    even = lax.rem(strip, 2) == 0
    rows, chans, width = guess_ref.shape
    lanes = lax.broadcasted_iota(jnp.int32, (chans, width), 1)
    first, last = lanes == 0, lanes == width - 1

    for ref in (xa_ref, xb_ref):
        ref[:, 3 * chans :, :] = jnp.zeros((ref.shape[0], ref.shape[1] - 3 * chans, width), jnp.bfloat16)
    band_ref[...] = jnp.zeros(band_ref.shape, jnp.bfloat16)
    head_ref[...] = jnp.zeros(head_ref.shape, jnp.bfloat16)

    parts = shift_ref[rows].astype(jnp.float32)
    line = parts[0:1] + parts[1:2] + parts[2:3]
    act = column(line[:, : proj_ref.shape[0]])
    terms = jnp.sum(act * proj_ref[...], axis=0, keepdims=True)
    biases = [cols_ref[0] + column(terms[:, :chans]), cols_ref[1], cols_ref[2]]
    cand_bias = cols_ref[3]
    gate_bias = cols_ref[4] + column(terms[:, chans:])
    skip = cols_ref[5]

    def put(ref, row, value):
        ref[row, :chans, :] = jnp.where(first, 0.0, pltpu.roll(value, 1, 1)).astype(jnp.bfloat16)
        ref[row, chans : 2 * chans, :] = value.astype(jnp.bfloat16)
        ref[row, 2 * chans : 3 * chans, :] = jnp.where(last, 0.0, pltpu.roll(value, width - 1, 1)).astype(jnp.bfloat16)

    for r in range(HALO):
        pair = pair_ref[r].astype(jnp.float32)
        chip = chip_ref[r].astype(jnp.float32)
        put(xa_ref, r, jnp.where(even, chip, pair))
        put(xa_ref, HALO + rows + r, jnp.where(even, pair, chip))
    for r in range(rows):
        put(xa_ref, HALO + r, guess_ref[r])

    def product(band, outs, src, g, n):
        k = (n + 2) * 128
        sides = [src[at : at + n + 2].reshape(k, width) for at in (g, g + n)]
        return jnp.dot(band[: n * outs, :k], jnp.concatenate(sides, axis=1), preferred_element_type=jnp.float32)

    top = strip == 0
    bottom = strip == lax.axis_size("space") - 1
    src, dst = xa_ref, xb_ref
    for layer in range(3):
        for r in range(GROUP):
            for a in range(3):
                band_ref[r * chans : (r + 1) * chans, (r + a) * 128 : (r + a + 1) * 128] = wh_ref[layer, a]
        halo = HALO - 1 - layer
        for g, n in groups_of(rows + 2 * halo):
            acc = product(band_ref, chans, src, g, n).reshape(n, chans, 2 * width)
            for j in range(2 * n):
                side = j // n
                pre = acc[j % n, :, side * width : (side + 1) * width] + biases[layer]
                value = 0.5 * pre * (1.0 + jnp.tanh(0.5 * pre))
                if g + j < halo:
                    value = jnp.where(top, 0.0, value)
                if g + j >= halo + rows:
                    value = jnp.where(bottom, 0.0, value)
                put(dst, g + j, value)
        src, dst = dst, src

    for r in range(GROUP):
        for a in range(3):
            head_ref[r * 2 * chans : (r + 1) * 2 * chans, (r + a) * 128 : (r + a + 1) * 128] = wo_ref[a]
    total = jnp.zeros((chans, width), jnp.float32)
    for g, n in groups_of(rows):
        acc = product(head_ref, 2 * chans, src, g, n).reshape(n, 2 * chans, 2 * width)
        for j in range(2 * n):
            row, side = g + j, j // n
            both = acc[j % n, :, side * width : (side + 1) * width]
            guess = guess_ref[row]
            cand = jnp.tanh(both[:chans] + cand_bias + skip * guess)
            rest = 1.0 / (1.0 + jnp.exp(both[chans:] + gate_bias))
            slope = (1.0 - cand * cand) * skip
            maps_ref[row, 0] = rest * (1.0 - slope)
            maps_ref[row, 1] = rest * (cand - slope * guess)
            fval = guess + rest * (cand - guess)
            diff = shift_ref[row].astype(jnp.float32) - fval
            total = total + diff * diff
    res_ref[...] = jnp.sum(total, axis=0, keepdims=True)


def prefix_kernel(maps_ref, pref_ref):
    shape = maps_ref.shape[2:]
    pref_ref[0, 0] = jnp.ones(shape, jnp.float32)
    pref_ref[0, 1] = jnp.zeros(shape, jnp.float32)
    a = 1.0 - maps_ref[0, 0]
    b = maps_ref[0, 1]
    for z in range(1, maps_ref.shape[0]):
        pref_ref[z, 0] = a
        pref_ref[z, 1] = b
        keep = 1.0 - maps_ref[z, 0]
        a, b = keep * a, keep * b + maps_ref[z, 1]


def params():
    return pltpu.CompilerParams(vmem_limit_bytes=LIMIT)


def body(traj, start_state, actions, hidden_w, hidden_b, head_w, cand_b, gate_b, skip, act_proj):
    _, chans, rows, width = traj.shape
    n_tm, n_space = lax.axis_size("tm"), lax.axis_size("space")
    place = lax.axis_index("tm")
    mine = place // NZ
    f32, bf16 = jnp.float32, jnp.bfloat16
    flat = traj.reshape(chans * rows, width)
    begin = start_state.reshape(chans * rows, width)

    loaded = (
        flat, begin, actions, hidden_b, cand_b[None], gate_b[None], skip[None], act_proj, hidden_w, jnp.swapaxes(head_w, 1, 2),
    )
    shift, pair, chip, guess, entry, cols, proj, taps, head_taps = pl.pallas_call(
        send_kernel,
        in_specs=[pl.BlockSpec(memory_space=pltpu.HBM)] * len(loaded),
        out_shape=(
            jax.ShapeDtypeStruct((rows + 1, chans, width), bf16),
            jax.ShapeDtypeStruct((HALO, chans, width), bf16),
            jax.ShapeDtypeStruct((HALO, chans, width), bf16),
            jax.ShapeDtypeStruct((rows, chans, width), f32),
            jax.ShapeDtypeStruct((chans, width), f32),
            jax.ShapeDtypeStruct((6, chans, width), f32),
            jax.ShapeDtypeStruct(act_proj.shape, f32),
            jax.ShapeDtypeStruct((3, 3, chans, 128), bf16),
            jax.ShapeDtypeStruct((3, 2 * chans, 128), bf16),
        ),
        scratch_shapes=[
            pltpu.VMEM((chans * rows, width), f32),
            pltpu.VMEM((chans * rows, width), f32),
            pltpu.VMEM(actions.shape, f32),
            pltpu.VMEM(hidden_b.shape, f32),
            pltpu.VMEM((1, chans), f32),
            pltpu.VMEM((1, chans), f32),
            pltpu.VMEM((1, chans), f32),
            pltpu.VMEM(hidden_w.shape, bf16),
            pltpu.VMEM((9, chans, 2 * chans), bf16),
            pltpu.VMEM((chans, width), f32),
            pltpu.SemaphoreType.DMA((len(loaded),)),
        ],
        compiler_params=params(),
        name="sends",
    )(*[pltpu.with_memory_space_constraint(value, pltpu.HBM) for value in loaded])
    crossing = [(s, s + 1) for s in range(1, n_space - 1, 2)]
    shift = lax.ppermute(shift, "tm", [((t + 1) % n_tm, t) for t in range(n_tm)])
    chip = lax.ppermute(chip, "space", crossing + [(b, a) for a, b in crossing])
    pair = lax.ppermute(pair, "space", [(s, s ^ 1) for s in range(n_space)])

    kb = (GROUP + 2) * 128
    maps, partial = pl.pallas_call(
        conv_kernel,
        out_shape=(
            jax.ShapeDtypeStruct((rows, 2, chans, width), f32),
            jax.ShapeDtypeStruct((1, width), f32),
        ),
        scratch_shapes=[
            pltpu.VMEM((rows + 2 * HALO, 128, width), bf16),
            pltpu.VMEM((rows + 2 * HALO, 128, width), bf16),
            pltpu.VMEM((GROUP * chans, kb), bf16),
            pltpu.VMEM((GROUP * 2 * chans, kb), bf16),
        ],
        compiler_params=params(),
        name="dynamics",
    )(guess, shift, pair, chip, proj, cols, taps, head_taps)

    z_groups = [[x * NZ + z for z in range(NZ)] for x in range(NX)]
    x_groups = [[x * NZ + z for x in range(NX)] for z in range(NZ)]
    sent = lax.all_to_all(maps.astype(jnp.float16), "tm", 0, 0, axis_index_groups=z_groups)
    for bit in (1, 2, 6):
        partial = partial + lax.ppermute(partial, "space", [(s, s ^ bit) for s in range(n_space)])
    flags = [mine == NX - 1] + [x < mine for x in range(NX - 1)]
    sent, partial, flags = lax.optimization_barrier((sent, partial, flags))

    steps = [(1.0 - sent[z, 0].astype(f32), sent[z, 1].astype(f32)) for z in range(NZ)]
    block_a, block_b = steps[0]
    for a, b in steps[1:]:
        block_a, block_b = a * block_a, a * block_b + b
    block = jnp.stack([jnp.where(flags[0], steps[-1][0], block_a), jnp.where(flags[0], steps[-1][1], block_b)])
    pref = pl.pallas_call(
        prefix_kernel,
        out_shape=jax.ShapeDtypeStruct((NZ, 2, chans, width), f32),
        compiler_params=params(),
        cost_estimate=pl.CostEstimate(flops=2**20, bytes_accessed=2**20, transcendentals=0),
        name="prefix",
    )(sent.astype(f32))
    copies, pref, entry = lax.optimization_barrier((jnp.broadcast_to(block[None], (NX,) + block.shape), pref, entry))
    blocks = lax.all_to_all(copies, "tm", 0, 0, axis_index_groups=x_groups)
    state = blocks[NX - 1, 0] * entry + blocks[NX - 1, 1]
    for x in range(NX - 1):
        state = jnp.where(flags[x + 1], blocks[x, 0] * state + blocks[x, 1], state)
    states = (pref[:, 0] * state + pref[:, 1]).astype(jnp.float16)
    back = lax.all_to_all(states, "tm", 0, 0, axis_index_groups=z_groups)
    partial = lax.ppermute(partial, "tm", [(t, (t + 1) % n_tm) for t in range(n_tm)])
    res_msq = jnp.sum(partial).reshape(1) / (chans * rows * width * n_space)
    back, res_msq = lax.optimization_barrier((back, res_msq))
    new_traj = jnp.swapaxes(back.astype(f32), 0, 1)[None]
    return new_traj, res_msq


def solution(mesh):
    return jax.shard_map(
        body,
        mesh=mesh,
        in_specs=(
            P("tm", None, "space", None),
            P(None, "space", None),
            P("tm", None),
            P(),
            P(),
            P(),
            P(),
            P(),
            P(),
            P(),
        ),
        out_specs=(P("tm", None, "space", None), P("tm")),
        check_vma=False,
    )
```

```python
import jax
import jax.numpy as jnp
from jax import lax
from jax.experimental import pallas as pl
from jax.experimental.pallas import tpu as pltpu
from jax.sharding import PartitionSpec as P


NX = 4
NZ = 16
HALO = 4
GROUP = 6
LIMIT = 16 * 2**20


def column(vec):
    n = vec.shape[1]
    rows = lax.broadcasted_iota(jnp.int32, (n, n), 0)
    cols = lax.broadcasted_iota(jnp.int32, (n, n), 1)
    return jnp.sum(jnp.where(rows == cols, jnp.broadcast_to(vec, (n, n)), 0.0), axis=1, keepdims=True)


def groups_of(rows):
    return [(g, min(GROUP, (rows - g) // 2)) for g in range(0, rows, 2 * GROUP)]


def rounded(value):
    return value.astype(jnp.bfloat16).astype(jnp.float32)


def send_kernel(
    traj_hbm, start_hbm, act_hbm, hb_hbm, cb_hbm, gb_hbm, sk_hbm, proj_hbm, wh_hbm, wo_hbm,
    shift_ref, pair_ref, chip_ref, traj_ref, start_ref, hb_ref, cb_ref, gb_ref, sk_ref, proj_ref, wh_ref, wo_ref,
    act_ref, line_ref, sems,
):
    chans, _ = shift_ref.shape[1:]
    rows = shift_ref.shape[0] - 1
    moves = [
        pltpu.make_async_copy(source, target, sems.at[i])
        for i, (source, target) in enumerate(
            (
                (traj_hbm, traj_ref),
                (start_hbm, start_ref),
                (act_hbm, act_ref),
                (hb_hbm, hb_ref),
                (cb_hbm, cb_ref),
                (gb_hbm, gb_ref),
                (sk_hbm, sk_ref),
                (proj_hbm, proj_ref),
                (wh_hbm, wh_ref),
                (wo_hbm, wo_ref),
            )
        )
    ]
    for move in moves:
        move.start()
    last = lax.axis_index("tm") == lax.axis_size("tm") - 1
    even = lax.rem(lax.axis_index("space"), 2) == 0
    line_ref[...] = jnp.zeros(line_ref.shape, jnp.float32)
    for move in moves:
        move.wait()
    rest = act_ref[...]
    for part in range(3):
        piece = rounded(rest)
        line_ref[part : part + 1, : piece.shape[1]] = piece
        rest = rest - piece
    shift_ref[rows] = line_ref[...].astype(jnp.bfloat16)
    for r in range(rows):
        shift_ref[r] = traj_ref[pl.ds(r, chans, stride=rows), :].astype(jnp.bfloat16)

    def guess(r):
        return jnp.where(last, start_ref[pl.ds(r, chans, stride=rows), :].astype(jnp.bfloat16), shift_ref[r])

    for r in range(HALO):
        upper, lower = guess(r), guess(rows - HALO + r)
        pair_ref[r] = jnp.where(even, lower, upper)
        chip_ref[r] = jnp.where(even, upper, lower)


def prep_kernel(
    traj_ref, start_ref, hb_ref, cb_ref, gb_ref, sk_ref, wh_ref, wo_ref,
    guess_ref, begin_ref, cols_ref, th_ref, to_ref,
):
    rows, chans, width = guess_ref.shape
    last = lax.axis_index("tm") == lax.axis_size("tm") - 1

    def spread(vec):
        return jnp.broadcast_to(column(vec), (chans, width))

    for i in range(3):
        cols_ref[i] = spread(hb_ref[i : i + 1, :])
    cols_ref[3] = spread(cb_ref[...])
    cols_ref[4] = spread(gb_ref[...])
    cols_ref[5] = spread(sk_ref[...])
    for r in range(rows):
        at = pl.ds(r, chans, stride=rows)
        guess_ref[r] = jnp.where(last, start_ref[at, :], traj_ref[at, :])
    place = lax.rem(lax.axis_index("tm"), NZ)
    begin_ref[...] = start_ref[pl.ds(place, chans, stride=rows), :]
    for a in range(3):
        for layer in range(3):
            th_ref[layer, a] = tile_of([wh_ref[layer, 3 * a + b].astype(jnp.float32) for b in range(3)])
        to_ref[a] = tile_of([wo_ref[3 * a + b].astype(jnp.float32).T for b in range(3)])


def tile_of(taps):
    outs, chans = taps[0].shape
    pad = jnp.zeros((outs, 128 - 3 * chans), jnp.float32)
    return jnp.concatenate(taps + [pad], axis=1).astype(jnp.bfloat16)


def conv_kernel(
    guess_ref, shift_ref, pair_ref, chip_ref, proj_ref, cols_ref, wh_ref, wo_ref,
    maps_ref, res_ref, xa_ref, xb_ref, band_ref, head_ref,
):
    strip = lax.axis_index("space")
    even = lax.rem(strip, 2) == 0
    rows, chans, width = guess_ref.shape
    lanes = lax.broadcasted_iota(jnp.int32, (chans, width), 1)
    first, last = lanes == 0, lanes == width - 1

    for ref in (xa_ref, xb_ref):
        ref[:, 3 * chans :, :] = jnp.zeros((ref.shape[0], ref.shape[1] - 3 * chans, width), jnp.bfloat16)
    band_ref[...] = jnp.zeros(band_ref.shape, jnp.bfloat16)
    head_ref[...] = jnp.zeros(head_ref.shape, jnp.bfloat16)

    parts = shift_ref[rows].astype(jnp.float32)
    line = parts[0:1] + parts[1:2] + parts[2:3]
    act = column(line[:, : proj_ref.shape[0]])
    terms = jnp.sum(act * proj_ref[...], axis=0, keepdims=True)
    biases = [cols_ref[0] + column(terms[:, :chans]), cols_ref[1], cols_ref[2]]
    cand_bias = cols_ref[3]
    gate_bias = cols_ref[4] + column(terms[:, chans:])
    skip = cols_ref[5]

    def put(ref, row, value):
        ref[row, :chans, :] = jnp.where(first, 0.0, pltpu.roll(value, 1, 1)).astype(jnp.bfloat16)
        ref[row, chans : 2 * chans, :] = value.astype(jnp.bfloat16)
        ref[row, 2 * chans : 3 * chans, :] = jnp.where(last, 0.0, pltpu.roll(value, width - 1, 1)).astype(jnp.bfloat16)

    for r in range(HALO):
        pair = pair_ref[r].astype(jnp.float32)
        chip = chip_ref[r].astype(jnp.float32)
        put(xa_ref, r, jnp.where(even, chip, pair))
        put(xa_ref, HALO + rows + r, jnp.where(even, pair, chip))
    for r in range(rows):
        put(xa_ref, HALO + r, guess_ref[r])

    def product(band, outs, src, g, n):
        k = (n + 2) * 128
        sides = [src[at : at + n + 2].reshape(k, width) for at in (g, g + n)]
        return jnp.dot(band[: n * outs, :k], jnp.concatenate(sides, axis=1), preferred_element_type=jnp.float32)

    top = strip == 0
    bottom = strip == lax.axis_size("space") - 1
    src, dst = xa_ref, xb_ref
    for layer in range(3):
        for r in range(GROUP):
            for a in range(3):
                band_ref[r * chans : (r + 1) * chans, (r + a) * 128 : (r + a + 1) * 128] = wh_ref[layer, a]
        halo = HALO - 1 - layer
        for g, n in groups_of(rows + 2 * halo):
            acc = product(band_ref, chans, src, g, n).reshape(n, chans, 2 * width)
            for j in range(2 * n):
                side = j // n
                pre = acc[j % n, :, side * width : (side + 1) * width] + biases[layer]
                value = 0.5 * pre * (1.0 + jnp.tanh(0.5 * pre))
                if g + j < halo:
                    value = jnp.where(top, 0.0, value)
                if g + j >= halo + rows:
                    value = jnp.where(bottom, 0.0, value)
                put(dst, g + j, value)
        src, dst = dst, src

    for r in range(GROUP):
        for a in range(3):
            head_ref[r * 2 * chans : (r + 1) * 2 * chans, (r + a) * 128 : (r + a + 1) * 128] = wo_ref[a]
    total = jnp.zeros((chans, width), jnp.float32)
    for g, n in groups_of(rows):
        acc = product(head_ref, 2 * chans, src, g, n).reshape(n, 2 * chans, 2 * width)
        for j in range(2 * n):
            row, side = g + j, j // n
            both = acc[j % n, :, side * width : (side + 1) * width]
            guess = guess_ref[row]
            cand = jnp.tanh(both[:chans] + cand_bias + skip * guess)
            rest = 1.0 / (1.0 + jnp.exp(both[chans:] + gate_bias))
            slope = (1.0 - cand * cand) * skip
            maps_ref[row, 0] = rest * (1.0 - slope)
            maps_ref[row, 1] = rest * (cand - slope * guess)
            fval = guess + rest * (cand - guess)
            diff = shift_ref[row].astype(jnp.float32) - fval
            total = total + diff * diff
    res_ref[...] = jnp.sum(total, axis=0, keepdims=True)


def prefix_kernel(maps_ref, pref_ref):
    shape = maps_ref.shape[2:]
    pref_ref[0, 0] = jnp.ones(shape, jnp.float32)
    pref_ref[0, 1] = jnp.zeros(shape, jnp.float32)
    a = 1.0 - maps_ref[0, 0]
    b = maps_ref[0, 1]
    for z in range(1, maps_ref.shape[0]):
        pref_ref[z, 0] = a
        pref_ref[z, 1] = b
        keep = 1.0 - maps_ref[z, 0]
        a, b = keep * a, keep * b + maps_ref[z, 1]


def params():
    return pltpu.CompilerParams(vmem_limit_bytes=LIMIT)


def body(traj, start_state, actions, hidden_w, hidden_b, head_w, cand_b, gate_b, skip, act_proj):
    _, chans, rows, width = traj.shape
    n_tm, n_space = lax.axis_size("tm"), lax.axis_size("space")
    place = lax.axis_index("tm")
    mine = place // NZ
    f32, bf16 = jnp.float32, jnp.bfloat16
    flat = traj.reshape(chans * rows, width)
    begin = start_state.reshape(chans * rows, width)

    loaded = (
        flat, begin, actions, hidden_b, cand_b[None], gate_b[None], skip[None], act_proj, hidden_w, jnp.swapaxes(head_w, 1, 2),
    )
    one = jax.ShapeDtypeStruct((1, chans), f32)
    shift, pair, chip, *kept = pl.pallas_call(
        send_kernel,
        in_specs=[pl.BlockSpec(memory_space=pltpu.HBM)] * len(loaded),
        out_shape=(
            jax.ShapeDtypeStruct((rows + 1, chans, width), bf16),
            jax.ShapeDtypeStruct((HALO, chans, width), bf16),
            jax.ShapeDtypeStruct((HALO, chans, width), bf16),
            jax.ShapeDtypeStruct((chans * rows, width), f32),
            jax.ShapeDtypeStruct((chans * rows, width), f32),
            jax.ShapeDtypeStruct(hidden_b.shape, f32),
            one,
            one,
            one,
            jax.ShapeDtypeStruct(act_proj.shape, f32),
            jax.ShapeDtypeStruct(hidden_w.shape, bf16),
            jax.ShapeDtypeStruct((9, chans, 2 * chans), bf16),
        ),
        scratch_shapes=[
            pltpu.VMEM(actions.shape, f32),
            pltpu.VMEM((chans, width), f32),
            pltpu.SemaphoreType.DMA((len(loaded),)),
        ],
        compiler_params=params(),
        name="sends",
    )(*[pltpu.with_memory_space_constraint(value, pltpu.HBM) for value in loaded])
    proj = kept.pop(6)
    guess, entry, cols, taps, head_taps = pl.pallas_call(
        prep_kernel,
        out_shape=(
            jax.ShapeDtypeStruct((rows, chans, width), f32),
            jax.ShapeDtypeStruct((chans, width), f32),
            jax.ShapeDtypeStruct((6, chans, width), f32),
            jax.ShapeDtypeStruct((3, 3, chans, 128), bf16),
            jax.ShapeDtypeStruct((3, 2 * chans, 128), bf16),
        ),
        compiler_params=params(),
        cost_estimate=pl.CostEstimate(flops=2**20, bytes_accessed=2**20, transcendentals=0),
        name="prep",
    )(*kept)
    crossing = [(s, s + 1) for s in range(1, n_space - 1, 2)]
    shift = lax.ppermute(shift, "tm", [((t + 1) % n_tm, t) for t in range(n_tm)])
    chip = lax.ppermute(chip, "space", crossing + [(b, a) for a, b in crossing])
    pair = lax.ppermute(pair, "space", [(s, s ^ 1) for s in range(n_space)])

    kb = (GROUP + 2) * 128
    maps, partial = pl.pallas_call(
        conv_kernel,
        out_shape=(
            jax.ShapeDtypeStruct((rows, 2, chans, width), f32),
            jax.ShapeDtypeStruct((1, width), f32),
        ),
        scratch_shapes=[
            pltpu.VMEM((rows + 2 * HALO, 128, width), bf16),
            pltpu.VMEM((rows + 2 * HALO, 128, width), bf16),
            pltpu.VMEM((GROUP * chans, kb), bf16),
            pltpu.VMEM((GROUP * 2 * chans, kb), bf16),
        ],
        compiler_params=params(),
        name="dynamics",
    )(guess, shift, pair, chip, proj, cols, taps, head_taps)

    z_groups = [[x * NZ + z for z in range(NZ)] for x in range(NX)]
    x_groups = [[x * NZ + z for x in range(NX)] for z in range(NZ)]
    sent = lax.all_to_all(maps.astype(jnp.float16), "tm", 0, 0, axis_index_groups=z_groups)
    for bit in (1, 2, 6):
        partial = partial + lax.ppermute(partial, "space", [(s, s ^ bit) for s in range(n_space)])
    flags = [mine == NX - 1] + [x < mine for x in range(NX - 1)]
    sent, partial, flags = lax.optimization_barrier((sent, partial, flags))

    steps = [(1.0 - sent[z, 0].astype(f32), sent[z, 1].astype(f32)) for z in range(NZ)]
    block_a, block_b = steps[0]
    for a, b in steps[1:]:
        block_a, block_b = a * block_a, a * block_b + b
    block = jnp.stack([jnp.where(flags[0], steps[-1][0], block_a), jnp.where(flags[0], steps[-1][1], block_b)])
    pref = pl.pallas_call(
        prefix_kernel,
        out_shape=jax.ShapeDtypeStruct((NZ, 2, chans, width), f32),
        compiler_params=params(),
        cost_estimate=pl.CostEstimate(flops=2**20, bytes_accessed=2**20, transcendentals=0),
        name="prefix",
    )(sent.astype(f32))
    copies, pref, entry = lax.optimization_barrier((jnp.broadcast_to(block.astype(jnp.float16)[None], (NX,) + block.shape), pref, entry))
    blocks = lax.all_to_all(copies, "tm", 0, 0, axis_index_groups=x_groups).astype(f32)
    state = blocks[NX - 1, 0] * entry + blocks[NX - 1, 1]
    for x in range(NX - 1):
        state = jnp.where(flags[x + 1], blocks[x, 0] * state + blocks[x, 1], state)
    states = (pref[:, 0] * state + pref[:, 1]).astype(jnp.float16)
    back = lax.all_to_all(states, "tm", 0, 0, axis_index_groups=z_groups)
    partial = lax.ppermute(partial, "tm", [(t, (t + 1) % n_tm) for t in range(n_tm)])
    res_msq = jnp.sum(partial).reshape(1) / (chans * rows * width * n_space)
    back, res_msq = lax.optimization_barrier((back, res_msq))
    new_traj = jnp.swapaxes(back.astype(f32), 0, 1)[None]
    return new_traj, res_msq


def solution(mesh):
    return jax.shard_map(
        body,
        mesh=mesh,
        in_specs=(
            P("tm", None, "space", None),
            P(None, "space", None),
            P("tm", None),
            P(),
            P(),
            P(),
            P(),
            P(),
            P(),
            P(),
        ),
        out_specs=(P("tm", None, "space", None), P("tm")),
        check_vma=False,
    )
```

```python
import jax
import jax.numpy as jnp
from jax import lax
from jax.experimental import pallas as pl
from jax.experimental.pallas import tpu as pltpu
from jax.sharding import PartitionSpec as P


PARTS = 4
HALO = 4
GROUP = 2
LIMIT = 16 * 2**20


def column(vec):
    n = vec.shape[1]
    rows = lax.broadcasted_iota(jnp.int32, (n, n), 0)
    cols = lax.broadcasted_iota(jnp.int32, (n, n), 1)
    return jnp.sum(jnp.where(rows == cols, jnp.broadcast_to(vec, (n, n)), 0.0), axis=1, keepdims=True)


def groups_of(rows):
    return [(g, min(GROUP, (rows - g) // 2)) for g in range(0, rows, 2 * GROUP)]


def rounded(value):
    return value.astype(jnp.bfloat16).astype(jnp.float32)


def send_kernel(
    traj_hbm, start_hbm, act_hbm, hb_hbm, cb_hbm, gb_hbm, sk_hbm, proj_hbm,
    shift_ref, pair_ref, chip_ref, traj_ref, start_ref, hb_ref, cb_ref, gb_ref, sk_ref, proj_ref,
    act_ref, line_ref, sems,
):
    chans, _ = shift_ref.shape[1:]
    rows = shift_ref.shape[0] - 1
    moves = [
        pltpu.make_async_copy(source, target, sems.at[i])
        for i, (source, target) in enumerate(
            (
                (traj_hbm, traj_ref),
                (start_hbm, start_ref),
                (act_hbm, act_ref),
                (hb_hbm, hb_ref),
                (cb_hbm, cb_ref),
                (gb_hbm, gb_ref),
                (sk_hbm, sk_ref),
                (proj_hbm, proj_ref),
            )
        )
    ]
    for move in moves:
        move.start()
    last = lax.axis_index("tm") == lax.axis_size("tm") - 1
    even = lax.rem(lax.axis_index("space"), 2) == 0
    line_ref[...] = jnp.zeros(line_ref.shape, jnp.float32)
    moves[0].wait()
    moves[2].wait()
    rest = act_ref[...]
    for part in range(3):
        piece = rounded(rest)
        line_ref[part : part + 1, : piece.shape[1]] = piece
        rest = rest - piece
    shift_ref[rows] = line_ref[...].astype(jnp.bfloat16)
    for r in range(rows):
        shift_ref[r] = traj_ref[pl.ds(r, chans, stride=rows), :].astype(jnp.bfloat16)

    moves[1].wait()

    def guess(r):
        return jnp.where(last, start_ref[pl.ds(r, chans, stride=rows), :].astype(jnp.bfloat16), shift_ref[r])

    for r in range(HALO):
        upper, lower = guess(r), guess(rows - HALO + r)
        pair_ref[r] = jnp.where(even, lower, upper)
        chip_ref[r] = jnp.where(even, upper, lower)
    for move in moves[3:]:
        move.wait()


def prep_kernel(
    traj_ref, start_ref, hb_ref, cb_ref, gb_ref, sk_ref, wh_ref, wo_ref,
    guess_ref, begin_ref, cols_ref, th_ref, to_ref,
):
    rows, chans, width = guess_ref.shape
    last = lax.axis_index("tm") == lax.axis_size("tm") - 1

    def spread(vec):
        return jnp.broadcast_to(column(vec), (chans, width))

    for i in range(3):
        cols_ref[i] = spread(hb_ref[i : i + 1, :])
    cols_ref[3] = spread(cb_ref[...])
    cols_ref[4] = spread(gb_ref[...])
    cols_ref[5] = spread(sk_ref[...])
    for r in range(rows):
        at = pl.ds(r, chans, stride=rows)
        guess_ref[r] = jnp.where(last, start_ref[at, :], traj_ref[at, :])
    place = lax.axis_index("tm")
    part = begin_ref.shape[0]
    first = lax.rem(place, PARTS) * (part * rows) + place // PARTS
    begin_ref[...] = start_ref[pl.ds(first, part, stride=rows), :]
    for a in range(3):
        for layer in range(3):
            th_ref[layer, a] = tile_of([wh_ref[layer, 3 * a + b].astype(jnp.float32) for b in range(3)])
        to_ref[a] = tile_of([wo_ref[3 * a + b].astype(jnp.float32).T for b in range(3)])


def tile_of(taps):
    outs, chans = taps[0].shape
    pad = jnp.zeros((outs, 128 - 3 * chans), jnp.float32)
    return jnp.concatenate(taps + [pad], axis=1).astype(jnp.bfloat16)


def conv_kernel(
    guess_ref, shift_ref, pair_ref, chip_ref, proj_ref, cols_ref, wh_ref, wo_ref,
    maps_ref, res_ref, xa_ref, xb_ref, band_ref, head_ref,
):
    strip = lax.axis_index("space")
    even = lax.rem(strip, 2) == 0
    rows, chans, width = guess_ref.shape
    lanes = lax.broadcasted_iota(jnp.int32, (chans, width), 1)
    first, last = lanes == 0, lanes == width - 1

    for ref in (xa_ref, xb_ref):
        ref[:, 3 * chans :, :] = jnp.zeros((ref.shape[0], ref.shape[1] - 3 * chans, width), jnp.bfloat16)
    band_ref[...] = jnp.zeros(band_ref.shape, jnp.bfloat16)
    head_ref[...] = jnp.zeros(head_ref.shape, jnp.bfloat16)

    parts = shift_ref[rows].astype(jnp.float32)
    line = parts[0:1] + parts[1:2] + parts[2:3]
    act = column(line[:, : proj_ref.shape[0]])
    terms = jnp.sum(act * proj_ref[...], axis=0, keepdims=True)
    biases = [cols_ref[0] + column(terms[:, :chans]), cols_ref[1], cols_ref[2]]
    cand_bias = cols_ref[3]
    gate_bias = cols_ref[4] + column(terms[:, chans:])
    skip = cols_ref[5]

    def put(ref, row, value):
        ref[row, :chans, :] = jnp.where(first, 0.0, pltpu.roll(value, 1, 1)).astype(jnp.bfloat16)
        ref[row, chans : 2 * chans, :] = value.astype(jnp.bfloat16)
        ref[row, 2 * chans : 3 * chans, :] = jnp.where(last, 0.0, pltpu.roll(value, width - 1, 1)).astype(jnp.bfloat16)

    for r in range(HALO):
        pair = pair_ref[r].astype(jnp.float32)
        chip = chip_ref[r].astype(jnp.float32)
        put(xa_ref, r, jnp.where(even, chip, pair))
        put(xa_ref, HALO + rows + r, jnp.where(even, pair, chip))
    for r in range(rows):
        put(xa_ref, HALO + r, guess_ref[r])

    def product(band, outs, src, g, n):
        k = (n + 2) * 128
        sides = [src[at : at + n + 2].reshape(k, width) for at in (g, g + n)]
        return jnp.dot(band[: n * outs, :k], jnp.concatenate(sides, axis=1), preferred_element_type=jnp.float32)

    top = strip == 0
    bottom = strip == lax.axis_size("space") - 1
    src, dst = xa_ref, xb_ref
    for layer in range(3):
        for r in range(GROUP):
            for a in range(3):
                band_ref[r * chans : (r + 1) * chans, (r + a) * 128 : (r + a + 1) * 128] = wh_ref[layer, a]
        halo = HALO - 1 - layer
        for g, n in groups_of(rows + 2 * halo):
            acc = product(band_ref, chans, src, g, n).reshape(n, chans, 2 * width)
            for j in range(2 * n):
                side = j // n
                pre = acc[j % n, :, side * width : (side + 1) * width] + biases[layer]
                value = 0.5 * pre * (1.0 + jnp.tanh(0.5 * pre))
                if g + j < halo:
                    value = jnp.where(top, 0.0, value)
                if g + j >= halo + rows:
                    value = jnp.where(bottom, 0.0, value)
                put(dst, g + j, value)
        src, dst = dst, src

    for r in range(GROUP):
        for a in range(3):
            head_ref[r * 2 * chans : (r + 1) * 2 * chans, (r + a) * 128 : (r + a + 1) * 128] = wo_ref[a]
    total = jnp.zeros((chans, width), jnp.float32)
    for g, n in groups_of(rows):
        acc = product(head_ref, 2 * chans, src, g, n).reshape(n, 2 * chans, 2 * width)
        for j in range(2 * n):
            row, side = g + j, j // n
            both = acc[j % n, :, side * width : (side + 1) * width]
            guess = guess_ref[row]
            cand = jnp.tanh(both[:chans] + cand_bias + skip * guess)
            rest = 1.0 / (1.0 + jnp.exp(both[chans:] + gate_bias))
            slope = (1.0 - cand * cand) * skip
            lost = rest * (1.0 - slope)
            offs = rest * (cand - slope * guess)
            for q in range(PARTS):
                at = slice(q * chans // PARTS, (q + 1) * chans // PARTS)
                maps_ref[row * PARTS + q, 0] = lost[at]
                maps_ref[row * PARTS + q, 1] = offs[at]
            fval = guess + rest * (cand - guess)
            diff = shift_ref[row].astype(jnp.float32) - fval
            total = total + diff * diff
    res_ref[...] = jnp.sum(total, axis=0, keepdims=True)


def scan_kernel(maps_ref, begin_ref, states_ref):
    steps = maps_ref.shape[0]
    state = begin_ref[...]
    for t in range(-1, steps - 1):
        at = t % steps
        state = state - maps_ref[at, 0] * state + maps_ref[at, 1]
        states_ref[t + 1] = state


def params():
    return pltpu.CompilerParams(vmem_limit_bytes=LIMIT)


def body(traj, start_state, actions, hidden_w, hidden_b, head_w, cand_b, gate_b, skip, act_proj):
    _, chans, rows, width = traj.shape
    n_tm, n_space = lax.axis_size("tm"), lax.axis_size("space")
    f32, bf16 = jnp.float32, jnp.bfloat16
    flat = traj.reshape(chans * rows, width)
    begin = start_state.reshape(chans * rows, width)

    loaded = (
        flat, begin, actions, hidden_b, cand_b[None], gate_b[None], skip[None], act_proj,
    )
    one = jax.ShapeDtypeStruct((1, chans), f32)
    shift, pair, chip, *kept = pl.pallas_call(
        send_kernel,
        in_specs=[pl.BlockSpec(memory_space=pltpu.HBM)] * len(loaded),
        out_shape=(
            jax.ShapeDtypeStruct((rows + 1, chans, width), bf16),
            jax.ShapeDtypeStruct((HALO, chans, width), bf16),
            jax.ShapeDtypeStruct((HALO, chans, width), bf16),
            jax.ShapeDtypeStruct((chans * rows, width), f32),
            jax.ShapeDtypeStruct((chans * rows, width), f32),
            jax.ShapeDtypeStruct(hidden_b.shape, f32),
            one,
            one,
            one,
            jax.ShapeDtypeStruct(act_proj.shape, f32),
        ),
        scratch_shapes=[
            pltpu.VMEM(actions.shape, f32),
            pltpu.VMEM((chans, width), f32),
            pltpu.SemaphoreType.DMA((len(loaded),)),
        ],
        compiler_params=params(),
        name="sends",
    )(*[pltpu.with_memory_space_constraint(value, pltpu.HBM) for value in loaded])
    proj = kept.pop(6)
    guess, entry, cols, taps, head_taps = pl.pallas_call(
        prep_kernel,
        out_shape=(
            jax.ShapeDtypeStruct((rows, chans, width), f32),
            jax.ShapeDtypeStruct((chans // PARTS, width), f32),
            jax.ShapeDtypeStruct((6, chans, width), f32),
            jax.ShapeDtypeStruct((3, 3, chans, 128), bf16),
            jax.ShapeDtypeStruct((3, 2 * chans, 128), bf16),
        ),
        compiler_params=params(),
        cost_estimate=pl.CostEstimate(flops=2**20, bytes_accessed=2**20, transcendentals=0),
        name="prep",
    )(*kept, hidden_w, jnp.swapaxes(head_w, 1, 2))
    crossing = [(s, s + 1) for s in range(1, n_space - 1, 2)]
    shift = lax.ppermute(shift, "tm", [((t + 1) % n_tm, t) for t in range(n_tm)])
    chip = lax.ppermute(chip, "space", crossing + [(b, a) for a, b in crossing])
    pair = lax.ppermute(pair, "space", [(s, s ^ 1) for s in range(n_space)])

    kb = (GROUP + 2) * 128
    maps, partial = pl.pallas_call(
        conv_kernel,
        out_shape=(
            jax.ShapeDtypeStruct((rows * PARTS, 2, chans // PARTS, width), f32),
            jax.ShapeDtypeStruct((1, width), f32),
        ),
        scratch_shapes=[
            pltpu.VMEM((rows + 2 * HALO, 128, width), bf16),
            pltpu.VMEM((rows + 2 * HALO, 128, width), bf16),
            pltpu.VMEM((GROUP * chans, kb), bf16),
            pltpu.VMEM((GROUP * 2 * chans, kb), bf16),
        ],
        compiler_params=params(),
        name="dynamics",
    )(guess, shift, pair, chip, proj, cols, taps, head_taps)

    sent = lax.all_to_all(maps.astype(jnp.float16), "tm", 0, 0)
    for bit in (1, 2, 6):
        partial = partial + lax.ppermute(partial, "space", [(s, s ^ bit) for s in range(n_space)])
    sent, partial = lax.optimization_barrier((sent, partial))
    states = pl.pallas_call(
        scan_kernel,
        out_shape=jax.ShapeDtypeStruct((n_tm, chans // PARTS, width), f32),
        compiler_params=params(),
        name="scan",
    )(sent.astype(f32), entry)
    back = lax.all_to_all(states.astype(jnp.float16), "tm", 0, 0)
    partial = lax.ppermute(partial, "tm", [(t, (t + 1) % n_tm) for t in range(n_tm)])
    res_msq = jnp.sum(partial).reshape(1) / (chans * rows * width * n_space)
    back, res_msq = lax.optimization_barrier((back, res_msq))
    back = back.reshape(rows, chans, width)
    new_traj = jnp.swapaxes(back.astype(f32), 0, 1)[None]
    return new_traj, res_msq


def solution(mesh):
    return jax.shard_map(
        body,
        mesh=mesh,
        in_specs=(
            P("tm", None, "space", None),
            P(None, "space", None),
            P("tm", None),
            P(),
            P(),
            P(),
            P(),
            P(),
            P(),
            P(),
        ),
        out_specs=(P("tm", None, "space", None), P("tm")),
        check_vma=False,
    )
```
